32 devices in a mesh: gz: 8 (over z, x), gy: 4 (over y, core).
Axes of the slice: x: 2, y: 2, z: 4, core: 2. Of those that a mesh axis runs over, the one named last changes fastest.
Arguments:
- iterate: float32 [16, 256, 1024], P('gz', 'gy'), may hold values from -1.5 to 1.5
- basis: bfloat16 [32, 16, 256, 1024], P(None, 'gz', 'gy'), may hold values from -6 to 6
- coeffs: float32 [32], replicated, may hold values from -0.3125 to 0.3125
- rhs: float32 [16, 256, 1024], P('gz', 'gy'), may hold values from -8 to 8
- kappa: float32 [16, 256, 1024], P('gz', 'gy'), may hold values from 0.5 to 4
- offsets: int32 [16, 256, 8], P('gz', 'gy'), may hold values from 0 to 2047
- flips: int32 [16, 256, 8], P('gz', 'gy'), may hold values from 0 to 1
Outputs:
- new_iterate: float32 [16, 256, 1024], P('gz', 'gy')
- residual: float32 [16, 256, 1024], P('gz', 'gy')
- sketch_unit: float32 [2048], replicated
The draws below stay inside these ranges and needn't reach their ends.
All inputs are finite; a program needn't handle non-finite values.
Results may differ from the reference program's by a relative error of at most 0.00058.
Values sent between devices are 32-bit elements; how exact they have to be, the bound alone decides.
A program may use at most 64 MiB of HBM per device.

```python
import math
import jax
import jax.numpy as jnp
from jax import lax

NX = 1024
KB = 32
SK = 2048
BLK = 128
NZ = 16
NY = 256


def plant(array, key, least, high):
    shape = array.shape
    spot = [jax.random.randint(jax.random.fold_in(key, axis), (), 0, shape[axis]) for axis in range(len(shape))]
    array = array.at[tuple(spot)].set(least)
    longest = shape.index(max(shape))
    spot[longest] = (spot[longest] + 1) % shape[longest]
    return array.at[tuple(spot)].set(high)


def block_scale(stream_key, dims, shards, low, high):
    def one(axis_at, shards_of):
        draws = jax.random.uniform(jax.random.fold_in(jax.random.fold_in(stream_key, 6), axis_at), (shards_of,), jnp.float32, low / len(shards), high / len(shards))
        return jnp.repeat(jnp.exp(draws), dims[axis_at] // shards_of).reshape((-1,) + (1,) * (len(dims) - axis_at - 1))

    gain = one(*shards[0])
    for cut in shards[1:]:
        gain = gain * one(*cut)
    return gain


def normal_values(rng, extent, scale, bound, shards=(), kind=jnp.bfloat16):
    loudness = block_scale(rng, extent, shards, -0.22, 0.18) if shards else 1.0
    drawn = jax.random.normal(rng, extent, jnp.float32) * scale * loudness
    return jnp.minimum(jnp.maximum(drawn, -bound), bound).astype(kind)


def setup_inputs(seed: int = 0) -> dict:
    keys = jax.random.split(jax.random.key(seed), 8)
    iterate = normal_values(keys[0], (NZ, NY, NX), 0.1, 1.5, ((0, 8), (1, 4)), jnp.float32)
    basis = normal_values(keys[1], (KB, NZ, NY, NX), 1.0, 6.0, ((1, 8), (2, 4)))
    coeffs = normal_values(keys[2], (KB,), 0.02, 0.3125, (), jnp.float32)
    rhs = normal_values(keys[3], (NZ, NY, NX), 1.0, 8.0, ((0, 8), (1, 4)), jnp.float32)
    kappa = jnp.clip(jnp.exp(math.log(4.0) - 2.0794415 * jax.random.uniform(keys[4], (NZ, NY, NX), jnp.float32) ** block_scale(keys[4], (NZ, NY, NX), ((0, 8), (1, 4)), -0.2, 0.2)), 0.5, 4.0)
    offsets = plant(jax.random.randint(keys[5], (NZ, NY, NX // BLK), 0, SK), jax.random.fold_in(keys[5], 1), 0, SK - 1).astype(jnp.int32)
    flips = plant(jax.random.randint(keys[6], (NZ, NY, NX // BLK), 0, 2), jax.random.fold_in(keys[6], 1), 0, 1).astype(jnp.int32)
    return {"iterate": iterate, "basis": basis, "coeffs": coeffs, "rhs": rhs, "kappa": kappa, "offsets": offsets, "flips": flips}


def apply_operator(upad, kpad):
    field = upad[1:-1, 1:-1, :]
    coef = kpad[1:-1, 1:-1, :]
    total = 0.05 * field
    neighbours = [(upad[2:, 1:-1, :], kpad[2:, 1:-1, :]), (upad[:-2, 1:-1, :], kpad[:-2, 1:-1, :]), (upad[1:-1, 2:, :], kpad[1:-1, 2:, :]), (upad[1:-1, :-2, :], kpad[1:-1, :-2, :])]
    zero_col = jnp.zeros_like(field[:, :, :1])
    neighbours.append((jnp.concatenate([field[:, :, 1:], zero_col], 2), jnp.concatenate([coef[:, :, 1:], zero_col], 2)))
    neighbours.append((jnp.concatenate([zero_col, field[:, :, :-1]], 2), jnp.concatenate([zero_col, coef[:, :, :-1]], 2)))
    for other, kother in neighbours:
        total = total + 0.5 * (coef + kother) * (field - other)
    return total

def reference(iterate, basis, coeffs, rhs, kappa, offsets, flips):
    coeff_b = lax.optimization_barrier(coeffs.astype(jnp.bfloat16)).astype(jnp.float32)

    def accumulate(index, acc):
        vector = lax.dynamic_index_in_dim(basis, index, 0, keepdims=False).astype(jnp.float32)
        return acc + coeff_b[index] * vector
    new_iterate = lax.fori_loop(0, KB, accumulate, iterate)
    widths = ((1, 1), (1, 1), (0, 0))
    operated = apply_operator(jnp.pad(new_iterate, widths), jnp.pad(kappa, widths))
    residual = rhs - operated
    blocks = residual.reshape(-1, BLK)
    signs = (2 * flips - 1).astype(jnp.float32).reshape(-1, 1)
    rows = (offsets.reshape(-1, 1) + jnp.arange(BLK, dtype=jnp.int32)[None, :]) % SK
    sketch = jax.ops.segment_sum((blocks * signs).reshape(-1), rows.reshape(-1).astype(jnp.int32), num_segments=SK)
    sketch_unit = sketch / jnp.sqrt(jnp.mean(sketch * sketch) + 1e-06)
    return (new_iterate, residual, sketch_unit)
```

```python
import functools

import jax
import jax.numpy as jnp
from jax import lax
from jax.experimental import pallas as pl
from jax.experimental.pallas import tpu as pltpu
from jax.sharding import PartitionSpec as P

SK = 2048
MESH = pl.DeviceIdType.MESH
F32 = jnp.float32
BF16 = jnp.bfloat16


def kernel(
    n_gz, n_gy, blk, rows,
    coef, iterate, basis, rhs, kappa, offsets, flips,
    u_out, r_out, s_out,
    bas, u, k, r, uh, kh, ysend, yrecv, slots_y, slots_z, part_y, part_z,
    bas_sem, load_sem, us, ur, ks, kr, ys, yr, s1s, s1r, s2s, s2r, out_sem, uout_sem,
):
    nk, nz, ny, nx = basis.shape
    nq = nx // blk
    step = 16
    nr = ny // step
    gz = lax.axis_index("gz")
    gy = lax.axis_index("gy")
    has_dn = gz > 0
    has_up = gz < n_gz - 1
    has_lf = gy > 0
    has_rt = gy < n_gy - 1
    planes = [nz - 1] + list(range(nz - 1))

    def bas_copy(z, c):
        rws = pl.ds(pl.multiple_of(c * step, step), step)
        return pltpu.make_async_copy(
            basis.at[:, z, rws, :], bas.at[:, z, rws, :], bas_sem.at[z, c]
        )

    u_load = pltpu.make_async_copy(iterate, u.at[:, pl.ds(8, ny), :], load_sem.at[0])
    k_load = pltpu.make_async_copy(kappa, k.at[:, pl.ds(8, ny), :], load_sem.at[1])
    r_load = pltpu.make_async_copy(rhs, r, load_sem.at[2])
    u_load.start()
    for c in range(nr):
        for z in planes:
            bas_copy(z, c).start()
    k_load.start()
    r_load.start()

    barrier = pltpu.get_barrier_semaphore()

    def hail(axis, me, count):
        def body(i, carry):
            pl.semaphore_signal(
                barrier, inc=1, device_id={axis: lax.rem(me + i, count)}, device_id_type=MESH
            )
            return carry
        lax.fori_loop(1, count, body, 0)

    hail("gz", gz, n_gz)
    hail("gy", gy, n_gy)
    pl.semaphore_wait(barrier, n_gz - 1 + n_gy - 1)

    up = {"gz": lax.rem(gz + 1, n_gz)}
    dn = {"gz": lax.rem(gz + n_gz - 1, n_gz)}
    rt = {"gy": lax.rem(gy + 1, n_gy)}
    lf = {"gy": lax.rem(gy + n_gy - 1, n_gy)}

    def remote(src, dst, ssem, rsem, dev):
        return pltpu.make_async_remote_copy(
            src_ref=src, dst_ref=dst, send_sem=ssem, recv_sem=rsem,
            device_id=dev, device_id_type=MESH,
        )

    def k_send(side):
        return remote(
            kappa.at[nz - 1 if side == 0 else 0], kh.at[side],
            ks.at[side], kr.at[side], up if side == 0 else dn,
        )

    def u_send(side, c):
        base = pl.multiple_of(c * step, step)
        return remote(
            u.at[nz - 1 if side == 0 else 0, pl.ds(8 + base, step), :],
            uh.at[side, pl.ds(base, step), :],
            us.at[side, c], ur.at[side, c], up if side == 0 else dn,
        )

    def y_send(side):
        return remote(
            ysend.at[side], yrecv.at[side], ys.at[side], yr.at[side],
            rt if side == 0 else lf,
        )

    z_out = (has_up, has_dn)
    z_in = (has_dn, has_up)
    y_out = (has_rt, has_lf)
    y_in = (has_lf, has_rt)
    for side in range(2):
        @pl.when(z_out[side])
        def _(side=side):
            k_send(side).start()

    u_load.wait()

    def combine(c, carry):
        for z in planes:
            base = pl.multiple_of(c * step, step)
            bas_copy(z, c).wait()
            acc = u[z, pl.ds(8 + base, step), :]
            for j in range(nk):
                acc = acc + coef[j] * bas[j, z, pl.ds(base, step), :].astype(F32)
            u[z, pl.ds(8 + base, step), :] = acc
            for side in range(2):
                if z == (nz - 1 if side == 0 else 0):
                    @pl.when(z_out[side])
                    def _(side=side):
                        u_send(side, c).start()
        return carry

    lax.fori_loop(0, nr, combine, 0)
    u_save = pltpu.make_async_copy(u.at[:, pl.ds(8, ny), :], u_out, uout_sem.at[0])
    u_save.start()
    k_load.wait()
    for side in range(2):
        row = 8 + (ny - 1 if side == 0 else 0)
        for z in range(nz):
            ysend[side, z : z + 1, :] = u[z, row : row + 1, :]
            ysend[side, nz + z : nz + z + 1, :] = k[z, row : row + 1, :]

        @pl.when(y_out[side])
        def _(side=side):
            y_send(side).start()

    for side in range(2):
        @pl.when(jnp.logical_not(z_in[side]))
        def _(side=side):
            uh[side] = jnp.zeros((ny, nx), F32)
            kh[side] = jnp.zeros((ny, nx), F32)

    r_load.wait()
    for side in range(2):
        row = 7 if side == 0 else 8 + ny

        @pl.when(y_in[side])
        def _(side=side, row=row):
            y_send(side).wait_recv()
            for z in range(nz):
                u[z, row : row + 1, :] = yrecv[side, z : z + 1, :]
                k[z, row : row + 1, :] = yrecv[side, nz + z : nz + z + 1, :]

        @pl.when(jnp.logical_not(y_in[side]))
        def _(row=row):
            for z in range(nz):
                u[z, row : row + 1, :] = jnp.zeros((1, nx), F32)
                k[z, row : row + 1, :] = jnp.zeros((1, nx), F32)

    lane = lax.broadcasted_iota(jnp.int32, (step, nx), 1)
    for c in range(nr):
        y0 = 8 + c * step
        for z in range(nz):
            uc = u[z, y0 : y0 + step, :]
            kc = k[z, y0 : y0 + step, :]

            def flux(ku, uu):
                return (kc + ku) * (uc - uu)

            ur_ = jnp.where(lane == nx - 1, 0.0, pltpu.roll(uc, nx - 1, 1))
            kr_ = jnp.where(lane == nx - 1, 0.0, pltpu.roll(kc, nx - 1, 1))
            fx = flux(kr_, ur_)
            tot = fx - jnp.where(lane == 0, -(kc * uc), pltpu.roll(fx, 1, 1))
            tot = tot + flux(k[z, y0 - 1 : y0 + step - 1, :], u[z, y0 - 1 : y0 + step - 1, :])
            tot = tot + flux(k[z, y0 + 1 : y0 + step + 1, :], u[z, y0 + 1 : y0 + step + 1, :])
            if z > 0:
                tot = tot + flux(k[z - 1, y0 : y0 + step, :], u[z - 1, y0 : y0 + step, :])
            if z < nz - 1:
                tot = tot + flux(k[z + 1, y0 : y0 + step, :], u[z + 1, y0 : y0 + step, :])
            sl = slice(c * step, (c + 1) * step)
            r[z, sl, :] = r[z, sl, :] - 0.05 * uc - 0.5 * tot

    for side in range(2):
        @pl.when(z_in[side])
        def _(side=side):
            k_send(side).wait_recv()

    col = lax.broadcasted_iota(jnp.int32, (step, blk), 1)

    def r_save(z, c):
        rws = pl.ds(pl.multiple_of(c * step, step), step)
        return pltpu.make_async_copy(r.at[z, rws, :], r_out.at[z, rws, :], out_sem.at[z, c])

    def finish(c, total):
        base = pl.multiple_of(c * step, step)
        rws = pl.ds(base, step)
        for side in range(2):
            @pl.when(z_in[side])
            def _(side=side):
                u_send(side, c).wait_recv()
        for z in range(nz):
            uc = u[z, pl.ds(8 + base, step), :]
            kc = k[z, pl.ds(8 + base, step), :]
            res = r[z, rws, :]
            if z == 0:
                res = res - 0.5 * ((kc + kh[0, rws, :]) * (uc - uh[0, rws, :]))
            if z == nz - 1:
                res = res - 0.5 * ((kc + kh[1, rws, :]) * (uc - uh[1, rws, :]))
            r[z, rws, :] = res
            r_save(z, c).start()
            off = offsets[pl.ds(pl.multiple_of(z * ny + base, step), step), :]
            flip = flips[pl.ds(pl.multiple_of(z * ny + base, step), step), :]
            sign = (2 * flip - 1).astype(F32)
            vals = []
            hots = []
            for q in range(nq):
                o = jnp.broadcast_to(off[:, q : q + 1], (step, blk))
                s = jnp.broadcast_to(sign[:, q : q + 1], (step, blk))
                x = res[:, q * blk : (q + 1) * blk] * s
                low = lax.rem(o, blk)
                bit = 1
                while bit < blk:
                    x = jnp.where((low & bit) != 0, pltpu.roll(x, bit, 1), x)
                    bit *= 2
                hi = o // blk
                nxt = jnp.where(hi == rows - 1, 0, hi + 1)
                keep = col >= low
                vals.append(jnp.where(keep, x, 0.0))
                vals.append(jnp.where(keep, 0.0, x))
                hots.append(jnp.where(col == hi, 1.0, 0.0).astype(BF16))
                hots.append(jnp.where(col == nxt, 1.0, 0.0).astype(BF16))
            val = jnp.concatenate(vals, 0)
            hot = jnp.concatenate(hots, 0)
            big = val.astype(BF16)
            small = (val - big.astype(F32)).astype(BF16)
            dims = (((0,), (0,)), ((), ()))
            total = total + lax.dot_general(hot, big, dims, preferred_element_type=F32)
            total = total + lax.dot_general(hot, small, dims, preferred_element_type=F32)
        return total

    total = lax.fori_loop(0, nr, finish, jnp.zeros((blk, blk), F32))

    def reduce(mine, axis, me, count, part, slots, ssem, rsem):
        part[...] = mine
        slots[me] = mine

        def send(i):
            dev = lax.rem(me + i, count)
            return remote(part, slots.at[me], ssem.at[i], rsem.at[me], {axis: dev})

        def take(i):
            src = lax.rem(me + i, count)
            return remote(part, slots.at[src], ssem.at[i], rsem.at[src], {axis: src})

        def go(i, carry):
            send(i).start()
            return carry

        def land(i, carry):
            take(i).wait_recv()
            return carry

        lax.fori_loop(1, count, go, 0)
        lax.fori_loop(1, count, land, 0)
        return lax.fori_loop(0, count, lambda i, acc: acc + slots[i], jnp.zeros_like(mine))

    total = reduce(total[:rows], "gy", gy, n_gy, part_y, slots_y, s1s, s1r)
    total = reduce(total, "gz", gz, n_gz, part_z, slots_z, s2s, s2r)
    mean = jnp.sum(total * total) / (rows * blk)
    s_out[...] = total / jnp.sqrt(jnp.full((rows, blk), mean, F32) + 1e-06)

    u_save.wait()
    for side in range(2):
        @pl.when(z_out[side])
        def _(side=side):
            k_send(side).wait_send()
            lax.fori_loop(0, nr, lambda c, x: (u_send(side, c).wait_send(), x)[1], 0)

        @pl.when(y_out[side])
        def _(side=side):
            y_send(side).wait_send()

    def drain(c, carry):
        for z in range(nz):
            r_save(z, c).wait()
        return carry

    lax.fori_loop(0, nr, drain, 0)

    def sent(axis, me, count, part, slots, ssem, rsem):
        def body(i, carry):
            dev = lax.rem(me + i, count)
            remote(part, slots.at[me], ssem.at[i], rsem.at[me], {axis: dev}).wait_send()
            return carry
        lax.fori_loop(1, count, body, 0)

    sent("gy", gy, n_gy, part_y, slots_y, s1s, s1r)
    sent("gz", gz, n_gz, part_z, slots_z, s2s, s2r)


def shards(n_gz, n_gy, iterate, basis, coeffs, rhs, kappa, offsets, flips):
    nk, nz, ny, nx = basis.shape
    nq = offsets.shape[-1]
    blk = nx // nq
    rows = SK // blk
    nr = ny // 16
    coef = lax.reduce_precision(coeffs, 8, 7)
    dma = pltpu.SemaphoreType.DMA
    hbm = pl.BlockSpec(memory_space=pl.ANY)
    vmem = pl.BlockSpec(memory_space=pltpu.VMEM)
    u, r, s = pl.pallas_call(
        functools.partial(kernel, n_gz, n_gy, blk, rows),
        out_shape=(
            jax.ShapeDtypeStruct((nz, ny, nx), F32),
            jax.ShapeDtypeStruct((nz, ny, nx), F32),
            jax.ShapeDtypeStruct((rows, blk), F32),
        ),
        in_specs=[pl.BlockSpec(memory_space=pltpu.SMEM), hbm, hbm, hbm, hbm, vmem, vmem],
        out_specs=(hbm, hbm, vmem),
        scratch_shapes=[
            pltpu.VMEM((nk, nz, ny, nx), BF16),
            pltpu.VMEM((nz, ny + 16, nx), F32),
            pltpu.VMEM((nz, ny + 16, nx), F32),
            pltpu.VMEM((nz, ny, nx), F32),
            pltpu.VMEM((2, ny, nx), F32),
            pltpu.VMEM((2, ny, nx), F32),
            pltpu.VMEM((2, 2 * nz, nx), F32),
            pltpu.VMEM((2, 2 * nz, nx), F32),
            pltpu.VMEM((n_gy, rows, blk), F32),
            pltpu.VMEM((n_gz, rows, blk), F32),
            pltpu.VMEM((rows, blk), F32),
            pltpu.VMEM((rows, blk), F32),
            dma((nz, nr)),
            dma((3,)),
            dma((2, nr)),
            dma((2, nr)),
            dma((2,)),
            dma((2,)),
            dma((2,)),
            dma((2,)),
            dma((n_gy,)),
            dma((n_gy,)),
            dma((n_gz,)),
            dma((n_gz,)),
            dma((nz, nr)),
            dma((1,)),
        ],
        compiler_params=pltpu.CompilerParams(collective_id=0, has_side_effects=True),
    )(
        coef, iterate, basis, rhs, kappa,
        offsets.reshape(nz * ny, nq), flips.reshape(nz * ny, nq),
    )
    return u, r, s.reshape(SK)


def solution(mesh):
    field = P("gz", "gy", None)
    return jax.shard_map(
        functools.partial(shards, mesh.shape["gz"], mesh.shape["gy"]),
        mesh=mesh,
        in_specs=(field, P(None, "gz", "gy", None), P(), field, field, field, field),
        out_specs=(field, field, P()),
        check_vma=False,
    )
```

```python
import functools

import jax
import jax.numpy as jnp
from jax import lax
from jax.experimental import pallas as pl
from jax.experimental.pallas import tpu as pltpu
from jax.sharding import PartitionSpec as P

SK = 2048
MESH = pl.DeviceIdType.MESH
F32 = jnp.float32
BF16 = jnp.bfloat16


def kernel(
    n_gz, n_gy, blk, rows,
    coef, iterate, basis, rhs, kappa, offsets, flips,
    u_out, r_out, s_out,
    bas, cf, u, k, r, uh, kh, tf, th, oh, offc, sgnc, ysend, yrecv,
    slots_y, slots_z, part_y, part_z,
    bas_sem, load_sem, us, ur, ks, kr, fs, fr, os_, or_, ys, yr, s1s, s1r, s2s, s2r,
    out_sem, uout_sem,
):
    nk, nz, ny, nx = basis.shape
    nq = nx // blk
    shift = blk.bit_length() - 1
    step = 16
    nr = ny // step
    half = nr // 2
    hrows = half * step
    assert nz >= 2 and ny == 2 * hrows and blk == 1 << shift
    gz = lax.axis_index("gz")
    gy = lax.axis_index("gy")
    has_dn = gz > 0
    has_up = gz < n_gz - 1
    has_lf = gy > 0
    has_rt = gy < n_gy - 1
    top = nz - 1

    def at(c):
        return pl.multiple_of(c * step, step)

    def bas_copy(z, c):
        rws = pl.ds(pl.multiple_of(c * step, step), step)
        return pltpu.make_async_copy(
            basis.at[:, z, rws, :], bas.at[:, z, rws, :], bas_sem.at[z, c]
        )

    u_load = pltpu.make_async_copy(iterate, u.at[:, pl.ds(8, ny), :], load_sem.at[0])
    k_load = pltpu.make_async_copy(kappa, k.at[:, pl.ds(8, ny), :], load_sem.at[1])
    r_load = pltpu.make_async_copy(rhs, r, load_sem.at[2])
    u_load.start()
    for i in range(half):
        bas_copy(top, i).start()
        bas_copy(0, half + i).start()
    for i in range(half):
        bas_copy(top, half + i).start()
        bas_copy(0, i).start()
        for z in range(1, top):
            bas_copy(z, i).start()
            bas_copy(z, half + i).start()
    k_load.start()
    r_load.start()

    barrier = pltpu.get_barrier_semaphore()

    def hail(axis, me, count):
        def body(i, carry):
            pl.semaphore_signal(
                barrier, inc=1, device_id={axis: lax.rem(me + i, count)}, device_id_type=MESH
            )
            return carry
        lax.fori_loop(1, count, body, 0)

    hail("gz", gz, n_gz)
    hail("gy", gy, n_gy)
    pl.semaphore_wait(barrier, n_gz - 1 + n_gy - 1)

    up = {"gz": lax.rem(gz + 1, n_gz)}
    dn = {"gz": lax.rem(gz + n_gz - 1, n_gz)}
    rt = {"gy": lax.rem(gy + 1, n_gy)}
    lf = {"gy": lax.rem(gy + n_gy - 1, n_gy)}

    def remote(src, dst, ssem, rsem, dev):
        return pltpu.make_async_remote_copy(
            src_ref=src, dst_ref=dst, send_sem=ssem, recv_sem=rsem,
            device_id=dev, device_id_type=MESH,
        )

    sent_plane = (top, 0)
    sent_row = (0, hrows)
    toward = (up, dn)

    def k_send(side):
        return remote(
            kappa.at[sent_plane[side], pl.ds(sent_row[side], hrows), :], kh.at[side],
            ks.at[side], kr.at[side], toward[side],
        )

    def o_send(side, which):
        src = (offsets, flips)[which]
        return remote(
            src.at[sent_plane[side]], oh.at[side, which],
            os_.at[side, which], or_.at[side, which], toward[side],
        )

    def u_send(side, i):
        return remote(
            u.at[sent_plane[side], pl.ds(8 + sent_row[side] + at(i), step), :],
            uh.at[side, pl.ds(at(i), step), :],
            us.at[side, i], ur.at[side, i], toward[side],
        )

    def f_send(side, i):
        return remote(
            tf.at[side, pl.ds(at(i), step), :], th.at[1 - side, pl.ds(at(i), step), :],
            fs.at[side, i], fr.at[1 - side, i], toward[1 - side],
        )

    def y_send(side):
        return remote(
            ysend.at[side], yrecv.at[side], ys.at[side], yr.at[side],
            rt if side == 0 else lf,
        )

    z_out = (has_up, has_dn)
    z_in = (has_dn, has_up)
    y_out = (has_rt, has_lf)
    y_in = (has_lf, has_rt)
    for side in range(2):
        @pl.when(z_out[side])
        def _(side=side):
            k_send(side).start()
            for which in range(2):
                o_send(side, which).start()

    for j in range(nk):
        cf[j] = jnp.full((step, blk), coef[j], F32).astype(BF16).astype(F32)
    u_load.wait()

    def combine(z, c):
        bas_copy(z, c).wait()
        acc = u[z, pl.ds(8 + at(c), step), :]
        for j in range(nk):
            cj = jnp.concatenate([cf[j]] * nq, 1)
            acc = acc + cj * bas[j, z, pl.ds(at(c), step), :].astype(F32)
        u[z, pl.ds(8 + at(c), step), :] = acc

    def first(i, carry):
        for side in range(2):
            combine(sent_plane[side], i + side * half)

            @pl.when(z_out[side])
            def _(side=side):
                u_send(side, i).start()
        return carry

    def second(i, carry):
        combine(top, half + i)
        combine(0, i)
        for z in range(1, top):
            combine(z, i)
            combine(z, half + i)
        return carry

    lax.fori_loop(0, half, first, 0)
    lax.fori_loop(0, half, second, 0)
    u_save = pltpu.make_async_copy(u.at[:, pl.ds(8, ny), :], u_out, uout_sem.at[0])
    u_save.start()
    k_load.wait()
    for side in range(2):
        row = 8 + (ny - 1 if side == 0 else 0)
        for z in range(nz):
            ysend[side, z : z + 1, :] = u[z, row : row + 1, :]
            ysend[side, nz + z : nz + z + 1, :] = k[z, row : row + 1, :]

        @pl.when(y_out[side])
        def _(side=side):
            y_send(side).start()

    for side in range(2):
        @pl.when(jnp.logical_not(z_in[side]))
        def _(side=side):
            uh[side] = jnp.zeros((hrows, nx), F32)
            kh[side] = jnp.zeros((hrows, nx), F32)
            th[side] = jnp.zeros((hrows, nx), F32)
            oh[side] = jnp.zeros((2, nq, ny), jnp.int32)

    r_load.wait()
    for side in range(2):
        row = 7 if side == 0 else 8 + ny

        @pl.when(y_in[side])
        def _(side=side, row=row):
            y_send(side).wait_recv()
            for z in range(nz):
                u[z, row : row + 1, :] = yrecv[side, z : z + 1, :]
                k[z, row : row + 1, :] = yrecv[side, nz + z : nz + z + 1, :]

        @pl.when(jnp.logical_not(y_in[side]))
        def _(row=row):
            for z in range(nz):
                u[z, row : row + 1, :] = jnp.zeros((1, nx), F32)
                k[z, row : row + 1, :] = jnp.zeros((1, nx), F32)

    lane = lax.broadcasted_iota(jnp.int32, (step, nx), 1)
    for c in range(nr):
        y0 = 8 + c * step
        for z in range(nz):
            uc = u[z, y0 : y0 + step, :]
            kc = k[z, y0 : y0 + step, :]

            def flux(ku, uu):
                return (kc + ku) * (uc - uu)

            ur_ = jnp.where(lane == nx - 1, 0.0, pltpu.roll(uc, nx - 1, 1))
            kr_ = jnp.where(lane == nx - 1, 0.0, pltpu.roll(kc, nx - 1, 1))
            fx = flux(kr_, ur_)
            tot = fx - jnp.where(lane == 0, -(kc * uc), pltpu.roll(fx, 1, 1))
            tot = tot + flux(k[z, y0 - 1 : y0 + step - 1, :], u[z, y0 - 1 : y0 + step - 1, :])
            tot = tot + flux(k[z, y0 + 1 : y0 + step + 1, :], u[z, y0 + 1 : y0 + step + 1, :])
            if z > 0:
                tot = tot + flux(k[z - 1, y0 : y0 + step, :], u[z - 1, y0 : y0 + step, :])
            if z < nz - 1:
                tot = tot + flux(k[z + 1, y0 : y0 + step, :], u[z + 1, y0 : y0 + step, :])
            sl = slice(c * step, (c + 1) * step)
            r[z, sl, :] = r[z, sl, :] - 0.05 * uc - 0.5 * tot

    for side in range(2):
        @pl.when(jnp.logical_not(z_in[side]))
        def _(side=side):
            z = (0, top)[side]
            row = hrows - sent_row[side]
            far = slice(row, row + hrows)
            beyond = slice(8 + row, 8 + row + hrows)
            r[z, far, :] = r[z, far, :] - 0.5 * (k[z, beyond, :] * u[z, beyond, :])

    def columns(p, off, flip):
        offc[p] = off.T
        sgnc[p] = (2 * flip - 1).astype(F32).T

    for z in range(nz):
        columns(z, offsets[z], flips[z])
    for side in range(2):
        @pl.when(z_in[side])
        def _(side=side):
            for which in range(2):
                o_send(side, which).wait_recv()
            k_send(side).wait_recv()
        columns(nz + side, oh[side, 0], oh[side, 1])

    col = lax.broadcasted_iota(jnp.int32, (step, blk), 1)

    def r_save(z, c):
        rws = pl.ds(at(c), step)
        return pltpu.make_async_copy(r.at[z, rws, :], r_out.at[z, rws, :], out_sem.at[z, c])

    def sketch(parts):
        vals = []
        hots = []
        for x_all, p, c in parts:
            off = offc[p, pl.ds(at(c), step), :]
            sgn = sgnc[p, pl.ds(at(c), step), :]
            for q in range(nq):
                o = jnp.broadcast_to(off[:, q : q + 1], (step, blk))
                s = jnp.broadcast_to(sgn[:, q : q + 1], (step, blk))
                x = x_all[:, q * blk : (q + 1) * blk] * s
                low = o & (blk - 1)
                bit = 1
                while bit < blk:
                    x = jnp.where((low & bit) != 0, pltpu.roll(x, bit, 1), x)
                    bit *= 2
                hi = lax.shift_right_logical(o, shift)
                nxt = jnp.where(hi == rows - 1, 0, hi + 1)
                keep = col >= low
                vals.append(jnp.where(keep, x, 0.0))
                vals.append(jnp.where(keep, 0.0, x))
                hots.append(jnp.where(col == hi, 1.0, 0.0).astype(BF16))
                hots.append(jnp.where(col == nxt, 1.0, 0.0).astype(BF16))
        val = jnp.concatenate(vals, 0)
        hot = jnp.concatenate(hots, 0)
        big = val.astype(BF16)
        small = (val - big.astype(F32)).astype(BF16)
        dims = (((0,), (0,)), ((), ()))
        return lax.dot_general(hot, big, dims, preferred_element_type=F32) + lax.dot_general(
            hot, small, dims, preferred_element_type=F32
        )

    def early(i, total):
        parts = [(r[top, pl.ds(at(i), step), :], top, i)]
        parts.append((r[0, pl.ds(at(half + i), step), :], 0, half + i))
        for z in range(1, top):
            for c in (i, half + i):
                parts.append((r[z, pl.ds(at(c), step), :], z, c))
                r_save(z, c).start()
        return total + sketch(parts)

    total = lax.fori_loop(0, half, early, jnp.zeros((blk, blk), F32))
    real = [jnp.where(z_in[side], 1.0, 0.0) for side in range(2)]

    def finish(i, total):
        parts = []
        for side in range(2):
            z = (0, top)[side]
            c = i + side * half

            @pl.when(z_in[side])
            def _(side=side):
                u_send(side, i).wait_recv()

            uc = u[z, pl.ds(8 + at(c), step), :]
            kc = k[z, pl.ds(8 + at(c), step), :]
            rws = pl.ds(at(i), step)
            t = 0.5 * ((kc + kh[side, rws, :]) * (uc - uh[side, rws, :]))
            tf[side, rws, :] = t

            @pl.when(z_in[side])
            def _(side=side):
                f_send(side, i).start()

            res = r[z, pl.ds(at(c), step), :] - t
            r[z, pl.ds(at(c), step), :] = res
            r_save(z, c).start()
            parts.append((res, z, c))
            parts.append((t * real[side], nz + side, c))
        return total + sketch(parts)

    total = lax.fori_loop(0, half, finish, total)

    def settle():
        def body(i, carry):
            for side in range(2):
                z = (0, top)[side]
                c = i + (1 - side) * half

                @pl.when(z_in[side])
                def _(side=side):
                    f_send(1 - side, i).wait_recv()

                rws = pl.ds(at(c), step)
                r[z, rws, :] = r[z, rws, :] + th[side, pl.ds(at(i), step), :]
                r_save(z, c).start()
            return carry
        lax.fori_loop(0, half, body, 0)

    def reduce(mine, axis, me, count, part, slots, ssem, rsem, between):
        part[...] = mine
        slots[me] = mine

        def send(i):
            dev = lax.rem(me + i, count)
            return remote(part, slots.at[me], ssem.at[i], rsem.at[me], {axis: dev})

        def take(i):
            src = lax.rem(me + i, count)
            return remote(part, slots.at[src], ssem.at[i], rsem.at[src], {axis: src})

        def go(i, carry):
            send(i).start()
            return carry

        def land(i, carry):
            take(i).wait_recv()
            return carry

        lax.fori_loop(1, count, go, 0)
        between()
        lax.fori_loop(1, count, land, 0)
        return lax.fori_loop(0, count, lambda i, acc: acc + slots[i], jnp.zeros_like(mine))

    total = reduce(total[:rows], "gy", gy, n_gy, part_y, slots_y, s1s, s1r, lambda: None)
    total = reduce(total, "gz", gz, n_gz, part_z, slots_z, s2s, s2r, settle)
    mean = jnp.sum(total * total) / (rows * blk)
    s_out[...] = total / jnp.sqrt(jnp.full((rows, blk), mean, F32) + 1e-06)

    u_save.wait()
    for side in range(2):
        @pl.when(z_out[side])
        def _(side=side):
            k_send(side).wait_send()
            for which in range(2):
                o_send(side, which).wait_send()
            lax.fori_loop(0, half, lambda i, x: (u_send(side, i).wait_send(), x)[1], 0)

        @pl.when(z_in[side])
        def _(side=side):
            lax.fori_loop(0, half, lambda i, x: (f_send(side, i).wait_send(), x)[1], 0)

        @pl.when(y_out[side])
        def _(side=side):
            y_send(side).wait_send()

    def drain(c, carry):
        for z in range(nz):
            r_save(z, c).wait()
        return carry

    lax.fori_loop(0, nr, drain, 0)

    def sent(axis, me, count, part, slots, ssem, rsem):
        def body(i, carry):
            dev = lax.rem(me + i, count)
            remote(part, slots.at[me], ssem.at[i], rsem.at[me], {axis: dev}).wait_send()
            return carry
        lax.fori_loop(1, count, body, 0)

    sent("gy", gy, n_gy, part_y, slots_y, s1s, s1r)
    sent("gz", gz, n_gz, part_z, slots_z, s2s, s2r)


def deliver(u_in, r_in, s_in, u_out, r_out, s_out, ub, rb, in_sem, out_sem):
    pairs = []
    nz, ny, nx = u_in.shape
    n = in_sem.shape[0] // 2
    for i in range(n):
        rws = pl.ds(i * (ny // n), ny // n)
        for j, (src, buf, dst) in enumerate(((u_in, ub, u_out), (r_in, rb, r_out))):
            sem = 2 * i + j
            pairs.append((
                pltpu.make_async_copy(src.at[:, rws, :], buf.at[:, rws, :], in_sem.at[sem]),
                pltpu.make_async_copy(buf.at[:, rws, :], dst.at[:, rws, :], out_sem.at[sem]),
            ))
    for load, _ in pairs:
        load.start()
    s_out[...] = s_in[...]
    for load, store in pairs:
        load.wait()
        store.start()
    for _, store in pairs:
        store.wait()


def shards(n_gz, n_gy, iterate, basis, coeffs, rhs, kappa, offsets, flips):
    nk, nz, ny, nx = basis.shape
    nq = offsets.shape[-1]
    blk = nx // nq
    rows = SK // blk
    nr = ny // 16
    half = nr // 2
    hrows = half * 16
    dma = pltpu.SemaphoreType.DMA
    hbm = pl.BlockSpec(memory_space=pl.ANY)
    vmem = pl.BlockSpec(memory_space=pltpu.VMEM)
    shapes = (
        jax.ShapeDtypeStruct((nz, ny, nx), F32),
        jax.ShapeDtypeStruct((nz, ny, nx), F32),
        jax.ShapeDtypeStruct((rows, blk), F32),
    )
    u, r, s = pl.pallas_call(
        functools.partial(kernel, n_gz, n_gy, blk, rows),
        out_shape=shapes,
        in_specs=[pl.BlockSpec(memory_space=pltpu.SMEM), hbm, hbm, hbm, hbm, vmem, vmem],
        out_specs=(hbm, hbm, vmem),
        scratch_shapes=[
            pltpu.VMEM((nk, nz, ny, nx), BF16),
            pltpu.VMEM((nk, 16, blk), F32),
            pltpu.VMEM((nz, ny + 16, nx), F32),
            pltpu.VMEM((nz, ny + 16, nx), F32),
            pltpu.VMEM((nz, ny, nx), F32),
            pltpu.VMEM((2, hrows, nx), F32),
            pltpu.VMEM((2, hrows, nx), F32),
            pltpu.VMEM((2, hrows, nx), F32),
            pltpu.VMEM((2, hrows, nx), F32),
            pltpu.VMEM((2, 2, nq, ny), jnp.int32),
            pltpu.VMEM((nz + 2, ny, nq), jnp.int32),
            pltpu.VMEM((nz + 2, ny, nq), F32),
            pltpu.VMEM((2, 2 * nz, nx), F32),
            pltpu.VMEM((2, 2 * nz, nx), F32),
            pltpu.VMEM((n_gy, rows, blk), F32),
            pltpu.VMEM((n_gz, rows, blk), F32),
            pltpu.VMEM((rows, blk), F32),
            pltpu.VMEM((rows, blk), F32),
            dma((nz, nr)),
            dma((3,)),
            dma((2, half)),
            dma((2, half)),
            dma((2,)),
            dma((2,)),
            dma((2, half)),
            dma((2, half)),
            dma((2, 2)),
            dma((2, 2)),
            dma((2,)),
            dma((2,)),
            dma((n_gy,)),
            dma((n_gy,)),
            dma((n_gz,)),
            dma((n_gz,)),
            dma((nz, nr)),
            dma((1,)),
        ],
        compiler_params=pltpu.CompilerParams(collective_id=0, has_side_effects=True),
    )(
        coeffs, iterate, basis, rhs, kappa,
        offsets.transpose(0, 2, 1), flips.transpose(0, 2, 1),
    )
    u, r, s = pl.pallas_call(
        deliver,
        out_shape=shapes,
        in_specs=[hbm, hbm, vmem],
        out_specs=(hbm, hbm, vmem),
        scratch_shapes=[
            pltpu.VMEM((nz, ny, nx), F32),
            pltpu.VMEM((nz, ny, nx), F32),
            dma((4,)),
            dma((4,)),
        ],
    )(u, r, s)
    return u, r, s.reshape(SK)


def solution(mesh):
    field = P("gz", "gy", None)
    return jax.shard_map(
        functools.partial(shards, mesh.shape["gz"], mesh.shape["gy"]),
        mesh=mesh,
        in_specs=(field, P(None, "gz", "gy", None), P(), field, field, field, field),
        out_specs=(field, field, P()),
        check_vma=False,
    )
```

```python
import functools

import jax
import jax.numpy as jnp
from jax import lax
from jax.experimental import pallas as pl
from jax.experimental.pallas import tpu as pltpu
from jax.sharding import PartitionSpec as P

SK = 2048
MESH = pl.DeviceIdType.MESH
F32 = jnp.float32
BF16 = jnp.bfloat16


def kernel(
    n_gz, n_gy, blk, rows,
    coef, iterate, basis, rhs, kappa, offsets, flips,
    u_out, r_out, s_out,
    bas, cf, u, k, r, uh, kh, tf, th, oh, lowb, hots, grid, ysend, yrecv,
    slots_y, slots_z, part_y, part_z,
    bas_sem, load_sem, us, ur, ks, kr, fs, fr, os_, or_, ys, yr, s1s, s1r, s2s, s2r,
    out_sem, uout_sem,
):
    nk, nz, ny, nx = basis.shape
    nq = nx // blk
    fine = 16
    cells = rows * blk // fine
    step = 16
    nr = ny // step
    half = nr // 2
    hrows = half * step
    assert nz >= 2 and ny == 2 * hrows and cells <= blk and blk % fine == 0
    gz = lax.axis_index("gz")
    gy = lax.axis_index("gy")
    has_dn = gz > 0
    has_up = gz < n_gz - 1
    has_lf = gy > 0
    has_rt = gy < n_gy - 1
    top = nz - 1

    def at(c):
        return pl.multiple_of(c * step, step)

    def bas_copy(z, c):
        rws = pl.ds(pl.multiple_of(c * step, step), step)
        return pltpu.make_async_copy(
            basis.at[:, z, rws, :], bas.at[:, z, rws, :], bas_sem.at[z, c]
        )

    u_load = pltpu.make_async_copy(iterate, u.at[:, pl.ds(8, ny), :], load_sem.at[0])
    k_load = pltpu.make_async_copy(kappa, k.at[:, pl.ds(8, ny), :], load_sem.at[1])
    r_load = pltpu.make_async_copy(rhs, r, load_sem.at[2])
    u_load.start()
    for i in range(half):
        bas_copy(top, i).start()
        bas_copy(0, half + i).start()
    for i in range(half):
        bas_copy(top, half + i).start()
        bas_copy(0, i).start()
        for z in range(1, top):
            bas_copy(z, i).start()
            bas_copy(z, half + i).start()
    k_load.start()
    r_load.start()

    barrier = pltpu.get_barrier_semaphore()

    def hail(axis, me, count):
        def body(i, carry):
            pl.semaphore_signal(
                barrier, inc=1, device_id={axis: lax.rem(me + i, count)}, device_id_type=MESH
            )
            return carry
        lax.fori_loop(1, count, body, 0)

    hail("gz", gz, n_gz)
    hail("gy", gy, n_gy)
    col = lax.broadcasted_iota(jnp.int32, (step, blk), 1)

    def prepare(p, off, flip, chunks):
        off = off.T
        sgn = (2 * flip - 1).astype(F32).T
        for c in chunks:
            rws = slice(c * step, (c + 1) * step)
            cols = []
            for q in range(nq):
                o = jnp.broadcast_to(off[rws, q : q + 1], (step, blk))
                s = jnp.broadcast_to(sgn[rws, q : q + 1], (step, blk))
                lowb[p, rws, q * blk : (q + 1) * blk] = o & (fine - 1)
                hi = o // fine
                nxt = hi + blk // fine
                nxt = jnp.where(nxt >= cells, nxt - cells, nxt)
                cols.append(jnp.where(col == hi, s, 0.0).astype(BF16))
                cols.append(jnp.where(col == nxt, s, 0.0).astype(BF16))
            hots[p, c] = jnp.concatenate(cols, 0).T

    for z in range(nz):
        prepare(z, offsets[z], flips[z], range(nr))
    for j in range(nk):
        cf[j] = jnp.full((step, blk), coef[j], F32).astype(BF16).astype(F32)
    pl.semaphore_wait(barrier, n_gz - 1 + n_gy - 1)

    up = {"gz": lax.rem(gz + 1, n_gz)}
    dn = {"gz": lax.rem(gz + n_gz - 1, n_gz)}
    rt = {"gy": lax.rem(gy + 1, n_gy)}
    lf = {"gy": lax.rem(gy + n_gy - 1, n_gy)}

    def remote(src, dst, ssem, rsem, dev):
        return pltpu.make_async_remote_copy(
            src_ref=src, dst_ref=dst, send_sem=ssem, recv_sem=rsem,
            device_id=dev, device_id_type=MESH,
        )

    sent_plane = (top, 0)
    sent_row = (0, hrows)
    toward = (up, dn)

    def k_send(side):
        return remote(
            kappa.at[sent_plane[side], pl.ds(sent_row[side], hrows), :], kh.at[side],
            ks.at[side], kr.at[side], toward[side],
        )

    def o_send(side, which):
        src = (offsets, flips)[which]
        return remote(
            src.at[sent_plane[side]], oh.at[side, which],
            os_.at[side, which], or_.at[side, which], toward[side],
        )

    def u_send(side, i):
        return remote(
            u.at[sent_plane[side], pl.ds(8 + sent_row[side] + at(i), step), :],
            uh.at[side, pl.ds(at(i), step), :],
            us.at[side, i], ur.at[side, i], toward[side],
        )

    def f_send(side, i):
        return remote(
            tf.at[side, pl.ds(at(i), step), :], th.at[1 - side, pl.ds(at(i), step), :],
            fs.at[side, i], fr.at[1 - side, i], toward[1 - side],
        )

    def y_send(side):
        return remote(
            ysend.at[side], yrecv.at[side], ys.at[side], yr.at[side],
            rt if side == 0 else lf,
        )

    z_out = (has_up, has_dn)
    z_in = (has_dn, has_up)
    y_out = (has_rt, has_lf)
    y_in = (has_lf, has_rt)
    for side in range(2):
        @pl.when(z_out[side])
        def _(side=side):
            k_send(side).start()
            for which in range(2):
                o_send(side, which).start()

    u_load.wait()

    def combine(z, c):
        bas_copy(z, c).wait()
        acc = u[z, pl.ds(8 + at(c), step), :]
        for j in range(nk):
            cj = jnp.concatenate([cf[j]] * nq, 1)
            acc = acc + cj * bas[j, z, pl.ds(at(c), step), :].astype(F32)
        u[z, pl.ds(8 + at(c), step), :] = acc

    def first(i, carry):
        for side in range(2):
            combine(sent_plane[side], i + side * half)

            @pl.when(z_out[side])
            def _(side=side):
                u_send(side, i).start()
        return carry

    def second(i, carry):
        combine(top, half + i)
        combine(0, i)
        for z in range(1, top):
            combine(z, i)
            combine(z, half + i)
        return carry

    lax.fori_loop(0, half, first, 0)
    lax.fori_loop(0, half, second, 0)
    u_save = pltpu.make_async_copy(u.at[:, pl.ds(8, ny), :], u_out, uout_sem.at[0])
    u_save.start()
    k_load.wait()
    for side in range(2):
        row = 8 + (ny - 1 if side == 0 else 0)
        for z in range(nz):
            ysend[side, z : z + 1, :] = u[z, row : row + 1, :]
            ysend[side, nz + z : nz + z + 1, :] = k[z, row : row + 1, :]

        @pl.when(y_out[side])
        def _(side=side):
            y_send(side).start()

    for side in range(2):
        @pl.when(jnp.logical_not(z_in[side]))
        def _(side=side):
            uh[side] = jnp.zeros((hrows, nx), F32)
            kh[side] = jnp.zeros((hrows, nx), F32)
            th[side] = jnp.zeros((hrows, nx), F32)
            oh[side] = jnp.zeros((2, nq, ny), jnp.int32)

    r_load.wait()
    for side in range(2):
        row = 7 if side == 0 else 8 + ny

        @pl.when(y_in[side])
        def _(side=side, row=row):
            y_send(side).wait_recv()
            for z in range(nz):
                u[z, row : row + 1, :] = yrecv[side, z : z + 1, :]
                k[z, row : row + 1, :] = yrecv[side, nz + z : nz + z + 1, :]

        @pl.when(jnp.logical_not(y_in[side]))
        def _(row=row):
            for z in range(nz):
                u[z, row : row + 1, :] = jnp.zeros((1, nx), F32)
                k[z, row : row + 1, :] = jnp.zeros((1, nx), F32)

    lane = lax.broadcasted_iota(jnp.int32, (step, nx), 1)
    for c in range(nr):
        y0 = 8 + c * step
        for z in range(nz):
            uc = u[z, y0 : y0 + step, :]
            kc = k[z, y0 : y0 + step, :]

            def flux(ku, uu):
                return (kc + ku) * (uc - uu)

            ur_ = jnp.where(lane == nx - 1, 0.0, pltpu.roll(uc, nx - 1, 1))
            kr_ = jnp.where(lane == nx - 1, 0.0, pltpu.roll(kc, nx - 1, 1))
            fx = flux(kr_, ur_)
            tot = fx - jnp.where(lane == 0, -(kc * uc), pltpu.roll(fx, 1, 1))
            tot = tot + flux(k[z, y0 - 1 : y0 + step - 1, :], u[z, y0 - 1 : y0 + step - 1, :])
            tot = tot + flux(k[z, y0 + 1 : y0 + step + 1, :], u[z, y0 + 1 : y0 + step + 1, :])
            if z > 0:
                tot = tot + flux(k[z - 1, y0 : y0 + step, :], u[z - 1, y0 : y0 + step, :])
            if z < nz - 1:
                tot = tot + flux(k[z + 1, y0 : y0 + step, :], u[z + 1, y0 : y0 + step, :])
            sl = slice(c * step, (c + 1) * step)
            r[z, sl, :] = r[z, sl, :] - 0.05 * uc - 0.5 * tot

    for side in range(2):
        @pl.when(jnp.logical_not(z_in[side]))
        def _(side=side):
            z = (0, top)[side]
            row = hrows - sent_row[side]
            far = slice(row, row + hrows)
            beyond = slice(8 + row, 8 + row + hrows)
            r[z, far, :] = r[z, far, :] - 0.5 * (k[z, beyond, :] * u[z, beyond, :])

    def r_save(z, c):
        rws = pl.ds(at(c), step)
        return pltpu.make_async_copy(r.at[z, rws, :], r_out.at[z, rws, :], out_sem.at[z, c])

    def sketch(parts):
        total = jnp.zeros((blk, blk), F32)
        for x_all, p, c in parts:
            vals = []
            for q in range(nq):
                x = x_all[:, q * blk : (q + 1) * blk]
                low = lowb[p, pl.ds(at(c), step), q * blk : (q + 1) * blk]
                bit = 1
                while bit < fine:
                    x = jnp.where((low & bit) != 0, pltpu.roll(x, bit, 1), x)
                    bit *= 2
                keep = col >= low
                vals.append(jnp.where(keep, x, 0.0))
                vals.append(jnp.where(keep, 0.0, x))
            val = jnp.concatenate(vals, 0)
            big = val.astype(BF16)
            small = (val - big.astype(F32)).astype(BF16)
            hot = hots[p, c]
            total = total + jnp.dot(hot, big, preferred_element_type=F32)
            total = total + jnp.dot(hot, small, preferred_element_type=F32)
        return total

    def early(i, total):
        parts = [(r[top, pl.ds(at(i), step), :], top, i)]
        parts.append((r[0, pl.ds(at(half + i), step), :], 0, half + i))
        for z in range(1, top):
            for c in (i, half + i):
                parts.append((r[z, pl.ds(at(c), step), :], z, c))
                r_save(z, c).start()
        return total + sketch(parts)

    total = lax.fori_loop(0, half, early, jnp.zeros((blk, blk), F32))
    real = [jnp.where(z_in[side], 1.0, 0.0) for side in range(2)]
    for side in range(2):
        @pl.when(z_in[side])
        def _(side=side):
            for which in range(2):
                o_send(side, which).wait_recv()
            k_send(side).wait_recv()
        prepare(nz + side, oh[side, 0], oh[side, 1], range(side * half, side * half + half))

    def finish(i, total):
        parts = []
        for side in range(2):
            z = (0, top)[side]
            c = i + side * half

            @pl.when(z_in[side])
            def _(side=side):
                u_send(side, i).wait_recv()

            uc = u[z, pl.ds(8 + at(c), step), :]
            kc = k[z, pl.ds(8 + at(c), step), :]
            rws = pl.ds(at(i), step)
            t = 0.5 * ((kc + kh[side, rws, :]) * (uc - uh[side, rws, :]))
            tf[side, rws, :] = t

            @pl.when(z_in[side])
            def _(side=side):
                f_send(side, i).start()

            res = r[z, pl.ds(at(c), step), :] - t
            r[z, pl.ds(at(c), step), :] = res
            r_save(z, c).start()
            parts.append((res, z, c))
            parts.append((t * real[side], nz + side, c))
        return total + sketch(parts)

    grid[...] = lax.fori_loop(0, half, finish, total)
    total = jnp.zeros((rows, blk), F32)
    lane = lax.broadcasted_iota(jnp.int32, (rows, blk), 1)
    for d in range(blk // fine):
        x = grid[pl.ds(d, rows, stride=blk // fine), :]
        x = pltpu.roll(x, d * fine, 1) if d else x
        total = total + jnp.where(lane >= d * fine, x, 0.0)
        if d:
            total = total + pltpu.roll(jnp.where(lane >= d * fine, 0.0, x), 1, 0)

    def settle():
        def body(i, carry):
            for side in range(2):
                z = (0, top)[side]
                c = i + (1 - side) * half

                @pl.when(z_in[side])
                def _(side=side):
                    f_send(1 - side, i).wait_recv()

                rws = pl.ds(at(c), step)
                r[z, rws, :] = r[z, rws, :] + th[side, pl.ds(at(i), step), :]
                r_save(z, c).start()
            return carry
        lax.fori_loop(0, half, body, 0)

    def reduce(mine, axis, me, count, part, slots, ssem, rsem, between):
        part[...] = mine
        slots[me] = mine

        def send(i):
            dev = lax.rem(me + i, count)
            return remote(part, slots.at[me], ssem.at[i], rsem.at[me], {axis: dev})

        def take(i):
            src = lax.rem(me + i, count)
            return remote(part, slots.at[src], ssem.at[i], rsem.at[src], {axis: src})

        def go(i, carry):
            send(i).start()
            return carry

        def land(i, carry):
            take(i).wait_recv()
            return carry

        lax.fori_loop(1, count, go, 0)
        between()
        lax.fori_loop(1, count, land, 0)
        return lax.fori_loop(0, count, lambda i, acc: acc + slots[i], jnp.zeros_like(mine))

    total = reduce(total, "gy", gy, n_gy, part_y, slots_y, s1s, s1r, lambda: None)
    total = reduce(total, "gz", gz, n_gz, part_z, slots_z, s2s, s2r, settle)
    mean = jnp.sum(total * total) / (rows * blk)
    s_out[...] = total / jnp.sqrt(jnp.full((rows, blk), mean, F32) + 1e-06)

    u_save.wait()
    for side in range(2):
        @pl.when(z_out[side])
        def _(side=side):
            k_send(side).wait_send()
            for which in range(2):
                o_send(side, which).wait_send()
            lax.fori_loop(0, half, lambda i, x: (u_send(side, i).wait_send(), x)[1], 0)

        @pl.when(z_in[side])
        def _(side=side):
            lax.fori_loop(0, half, lambda i, x: (f_send(side, i).wait_send(), x)[1], 0)

        @pl.when(y_out[side])
        def _(side=side):
            y_send(side).wait_send()

    def drain(c, carry):
        for z in range(nz):
            r_save(z, c).wait()
        return carry

    lax.fori_loop(0, nr, drain, 0)

    def sent(axis, me, count, part, slots, ssem, rsem):
        def body(i, carry):
            dev = lax.rem(me + i, count)
            remote(part, slots.at[me], ssem.at[i], rsem.at[me], {axis: dev}).wait_send()
            return carry
        lax.fori_loop(1, count, body, 0)

    sent("gy", gy, n_gy, part_y, slots_y, s1s, s1r)
    sent("gz", gz, n_gz, part_z, slots_z, s2s, s2r)


def deliver(u_in, r_in, s_in, u_out, r_out, s_out, ub, rb, in_sem, out_sem):
    pairs = []
    nz, ny, nx = u_in.shape
    n = in_sem.shape[0] // 2
    for i in range(n):
        rws = pl.ds(i * (ny // n), ny // n)
        for j, (src, buf, dst) in enumerate(((u_in, ub, u_out), (r_in, rb, r_out))):
            sem = 2 * i + j
            pairs.append((
                pltpu.make_async_copy(src.at[:, rws, :], buf.at[:, rws, :], in_sem.at[sem]),
                pltpu.make_async_copy(buf.at[:, rws, :], dst.at[:, rws, :], out_sem.at[sem]),
            ))
    for load, _ in pairs:
        load.start()
    s_out[...] = s_in[...]
    for load, store in pairs:
        load.wait()
        store.start()
    for _, store in pairs:
        store.wait()


def shards(n_gz, n_gy, iterate, basis, coeffs, rhs, kappa, offsets, flips):
    nk, nz, ny, nx = basis.shape
    nq = offsets.shape[-1]
    blk = nx // nq
    rows = SK // blk
    nr = ny // 16
    half = nr // 2
    hrows = half * 16
    dma = pltpu.SemaphoreType.DMA
    hbm = pl.BlockSpec(memory_space=pl.ANY)
    vmem = pl.BlockSpec(memory_space=pltpu.VMEM)
    shapes = (
        jax.ShapeDtypeStruct((nz, ny, nx), F32),
        jax.ShapeDtypeStruct((nz, ny, nx), F32),
        jax.ShapeDtypeStruct((rows, blk), F32),
    )
    u, r, s = pl.pallas_call(
        functools.partial(kernel, n_gz, n_gy, blk, rows),
        out_shape=shapes,
        in_specs=[pl.BlockSpec(memory_space=pltpu.SMEM), hbm, hbm, hbm, hbm, vmem, vmem],
        out_specs=(hbm, hbm, vmem),
        scratch_shapes=[
            pltpu.VMEM((nk, nz, ny, nx), BF16),
            pltpu.VMEM((nk, 16, blk), F32),
            pltpu.VMEM((nz, ny + 16, nx), F32),
            pltpu.VMEM((nz, ny + 16, nx), F32),
            pltpu.VMEM((nz, ny, nx), F32),
            pltpu.VMEM((2, hrows, nx), F32),
            pltpu.VMEM((2, hrows, nx), F32),
            pltpu.VMEM((2, hrows, nx), F32),
            pltpu.VMEM((2, hrows, nx), F32),
            pltpu.VMEM((2, 2, nq, ny), jnp.int32),
            pltpu.VMEM((nz + 2, ny, nx), jnp.int32),
            pltpu.VMEM((nz + 2, nr, blk, 2 * nq * 16), BF16),
            pltpu.VMEM((blk, blk), F32),
            pltpu.VMEM((2, 2 * nz, nx), F32),
            pltpu.VMEM((2, 2 * nz, nx), F32),
            pltpu.VMEM((n_gy, rows, blk), F32),
            pltpu.VMEM((n_gz, rows, blk), F32),
            pltpu.VMEM((rows, blk), F32),
            pltpu.VMEM((rows, blk), F32),
            dma((nz, nr)),
            dma((3,)),
            dma((2, half)),
            dma((2, half)),
            dma((2,)),
            dma((2,)),
            dma((2, half)),
            dma((2, half)),
            dma((2, 2)),
            dma((2, 2)),
            dma((2,)),
            dma((2,)),
            dma((n_gy,)),
            dma((n_gy,)),
            dma((n_gz,)),
            dma((n_gz,)),
            dma((nz, nr)),
            dma((1,)),
        ],
        compiler_params=pltpu.CompilerParams(collective_id=0, has_side_effects=True),
    )(
        coeffs, iterate, basis, rhs, kappa,
        offsets.transpose(0, 2, 1), flips.transpose(0, 2, 1),
    )
    u, r, s = pl.pallas_call(
        deliver,
        out_shape=shapes,
        in_specs=[hbm, hbm, vmem],
        out_specs=(hbm, hbm, vmem),
        scratch_shapes=[
            pltpu.VMEM((nz, ny, nx), F32),
            pltpu.VMEM((nz, ny, nx), F32),
            dma((4,)),
            dma((4,)),
        ],
    )(u, r, s)
    return u, r, s.reshape(SK)


def solution(mesh):
    field = P("gz", "gy", None)
    return jax.shard_map(
        functools.partial(shards, mesh.shape["gz"], mesh.shape["gy"]),
        mesh=mesh,
        in_specs=(field, P(None, "gz", "gy", None), P(), field, field, field, field),
        out_specs=(field, field, P()),
        check_vma=False,
    )
```

```python
import functools

import jax
import jax.numpy as jnp
from jax import lax
from jax.experimental import pallas as pl
from jax.experimental.pallas import tpu as pltpu
from jax.sharding import PartitionSpec as P

SK = 2048
MESH = pl.DeviceIdType.MESH
F32 = jnp.float32
BF16 = jnp.bfloat16


def kernel(
    n_gz, n_gy, blk, rows,
    coef, iterate, basis, rhs, kappa, offsets, flips,
    u_out, r_out, s_out,
    bas, cf, u, k, r, uh, kh, tf, th, oh, lowb, hots, grid, ysend, yrecv,
    slots_y, slots_z, part_y, part_z,
    bas_sem, load_sem, us, ur, ks, kr, fs, fr, os_, or_, ys, yr, s1s, s1r, s2s, s2r,
    out_sem, uout_sem, near,
):
    nk, nz, ny, nx = basis.shape
    nq = nx // blk
    fine = 16
    cells = rows * blk // fine
    step = 16
    nr = ny // step
    half = nr // 2
    hrows = half * step
    assert nz >= 2 and ny == 2 * hrows and cells <= blk and blk % fine == 0
    gz = lax.axis_index("gz")
    gy = lax.axis_index("gy")
    has_dn = gz > 0
    has_up = gz < n_gz - 1
    has_lf = gy > 0
    has_rt = gy < n_gy - 1
    top = nz - 1

    def at(c):
        return pl.multiple_of(c * step, step)

    def bas_copy(z, c):
        rws = pl.ds(pl.multiple_of(c * step, step), step)
        return pltpu.make_async_copy(
            basis.at[:, z, rws, :], bas.at[:, z, rws, :], bas_sem.at[z, c]
        )

    u_load = pltpu.make_async_copy(iterate, u.at[:, pl.ds(8, ny), :], load_sem.at[0])
    k_load = pltpu.make_async_copy(kappa, k.at[:, pl.ds(8, ny), :], load_sem.at[1])
    r_load = pltpu.make_async_copy(rhs, r, load_sem.at[2])
    u_load.start()
    for i in range(half):
        bas_copy(top, i).start()
        bas_copy(0, half + i).start()
    for i in range(half):
        bas_copy(top, half + i).start()
        bas_copy(0, i).start()
        for z in range(1, top):
            bas_copy(z, i).start()
            bas_copy(z, half + i).start()
    k_load.start()
    r_load.start()

    barrier = pltpu.get_barrier_semaphore()

    def hail(axis, me, count):
        def body(i, carry):
            pl.semaphore_signal(
                barrier, inc=1, device_id={axis: lax.rem(me + i, count)}, device_id_type=MESH
            )
            return carry
        lax.fori_loop(1, count, body, 0)

    def tell(side, sem):
        @pl.when((has_up, has_dn)[side])
        def _():
            dev = lax.rem(gz + (1, n_gz - 1)[side], n_gz)
            pl.semaphore_signal(sem, inc=1, device_id={"gz": dev}, device_id_type=MESH)

    for side in range(2):
        tell(side, barrier)
    hail("gy", gy, n_gy)
    col = lax.broadcasted_iota(jnp.int32, (step, blk), 1)

    def prepare(p, off, flip, chunks):
        off = off.T
        sgn = (2 * flip - 1).astype(F32).T
        for c in chunks:
            rws = slice(c * step, (c + 1) * step)
            cols = []
            for q in range(nq):
                o = jnp.broadcast_to(off[rws, q : q + 1], (step, blk))
                s = jnp.broadcast_to(sgn[rws, q : q + 1], (step, blk))
                lowb[p, rws, q * blk : (q + 1) * blk] = o & (fine - 1)
                hi = o // fine
                nxt = hi + blk // fine
                nxt = jnp.where(nxt >= cells, nxt - cells, nxt)
                cols.append(jnp.where(col == hi, s, 0.0).astype(BF16))
                cols.append(jnp.where(col == nxt, s, 0.0).astype(BF16))
            hots[p, c] = jnp.concatenate(cols, 0).T

    for j in range(nk):
        cf[j] = jnp.full((step, blk), coef[j], F32).astype(BF16).astype(F32)
    pl.semaphore_wait(barrier, n_gy - 1 + has_up.astype(jnp.int32) + has_dn.astype(jnp.int32))

    rounds = max(n_gz - 2, 0)

    def speak(t):
        for side in range(2):
            tell(side, near.at[side, t])

    def hear(t):
        for side in range(2):
            @pl.when((has_dn, has_up)[side])
            def _(side=side):
                pl.semaphore_wait(near.at[side, t], 1)

    state = {"said": 0, "heard": 0}

    def gossip():
        if state["heard"] < state["said"]:
            hear(state["heard"])
            state["heard"] += 1
        if state["said"] < rounds:
            speak(state["said"])
            state["said"] += 1


    up = {"gz": lax.rem(gz + 1, n_gz)}
    dn = {"gz": lax.rem(gz + n_gz - 1, n_gz)}
    rt = {"gy": lax.rem(gy + 1, n_gy)}
    lf = {"gy": lax.rem(gy + n_gy - 1, n_gy)}

    def remote(src, dst, ssem, rsem, dev):
        return pltpu.make_async_remote_copy(
            src_ref=src, dst_ref=dst, send_sem=ssem, recv_sem=rsem,
            device_id=dev, device_id_type=MESH,
        )

    sent_plane = (top, 0)
    sent_row = (0, hrows)
    toward = (up, dn)

    def k_send(side):
        return remote(
            kappa.at[sent_plane[side], pl.ds(sent_row[side], hrows), :], kh.at[side],
            ks.at[side], kr.at[side], toward[side],
        )

    def o_send(side, which):
        src = (offsets, flips)[which]
        return remote(
            src.at[sent_plane[side]], oh.at[side, which],
            os_.at[side, which], or_.at[side, which], toward[side],
        )

    def u_send(side, i):
        return remote(
            u.at[sent_plane[side], pl.ds(8 + sent_row[side] + at(i), step), :],
            uh.at[side, pl.ds(at(i), step), :],
            us.at[side, i], ur.at[side, i], toward[side],
        )

    def f_send(side, i):
        return remote(
            tf.at[side, pl.ds(at(i), step), :], th.at[1 - side, pl.ds(at(i), step), :],
            fs.at[side, i], fr.at[1 - side, i], toward[1 - side],
        )

    def y_send(side):
        return remote(
            ysend.at[side], yrecv.at[side], ys.at[side], yr.at[side],
            rt if side == 0 else lf,
        )

    z_out = (has_up, has_dn)
    z_in = (has_dn, has_up)
    y_out = (has_rt, has_lf)
    y_in = (has_lf, has_rt)
    for side in range(2):
        @pl.when(z_out[side])
        def _(side=side):
            k_send(side).start()
            for which in range(2):
                o_send(side, which).start()

    gossip()

    u_load.wait()

    def combine(z, c):
        bas_copy(z, c).wait()
        acc = u[z, pl.ds(8 + at(c), step), :]
        for j in range(nk):
            cj = jnp.concatenate([cf[j]] * nq, 1)
            acc = acc + cj * bas[j, z, pl.ds(at(c), step), :].astype(F32)
        u[z, pl.ds(8 + at(c), step), :] = acc

    def first(i, carry):
        for side in range(2):
            combine(sent_plane[side], i + side * half)

            @pl.when(z_out[side])
            def _(side=side):
                u_send(side, i).start()
        return carry

    def second(i, carry):
        combine(top, half + i)
        combine(0, i)
        for z in range(1, top):
            combine(z, i)
            combine(z, half + i)
        return carry

    lax.fori_loop(0, half, first, 0)
    gossip()
    lax.fori_loop(0, half, second, 0)
    gossip()
    u_save = pltpu.make_async_copy(u.at[:, pl.ds(8, ny), :], u_out, uout_sem.at[0])
    u_save.start()
    k_load.wait()
    for side in range(2):
        row = 8 + (ny - 1 if side == 0 else 0)
        for z in range(nz):
            ysend[side, z : z + 1, :] = u[z, row : row + 1, :]
            ysend[side, nz + z : nz + z + 1, :] = k[z, row : row + 1, :]

        @pl.when(y_out[side])
        def _(side=side):
            y_send(side).start()

    for side in range(2):
        @pl.when(jnp.logical_not(z_in[side]))
        def _(side=side):
            uh[side] = jnp.zeros((hrows, nx), F32)
            kh[side] = jnp.zeros((hrows, nx), F32)
            th[side] = jnp.zeros((hrows, nx), F32)
            oh[side] = jnp.zeros((2, nq, ny), jnp.int32)

    r_load.wait()
    for side in range(2):
        row = 7 if side == 0 else 8 + ny

        @pl.when(y_in[side])
        def _(side=side, row=row):
            y_send(side).wait_recv()
            for z in range(nz):
                u[z, row : row + 1, :] = yrecv[side, z : z + 1, :]
                k[z, row : row + 1, :] = yrecv[side, nz + z : nz + z + 1, :]

        @pl.when(jnp.logical_not(y_in[side]))
        def _(row=row):
            for z in range(nz):
                u[z, row : row + 1, :] = jnp.zeros((1, nx), F32)
                k[z, row : row + 1, :] = jnp.zeros((1, nx), F32)

    for z in range(nz):
        prepare(z, offsets[z], flips[z], range(nr))
    gossip()
    lane = lax.broadcasted_iota(jnp.int32, (step, nx), 1)
    for c in range(nr):
        y0 = 8 + c * step
        for z in range(nz):
            uc = u[z, y0 : y0 + step, :]
            kc = k[z, y0 : y0 + step, :]

            def flux(ku, uu):
                return (kc + ku) * (uc - uu)

            ur_ = jnp.where(lane == nx - 1, 0.0, pltpu.roll(uc, nx - 1, 1))
            kr_ = jnp.where(lane == nx - 1, 0.0, pltpu.roll(kc, nx - 1, 1))
            fx = flux(kr_, ur_)
            tot = fx - jnp.where(lane == 0, -(kc * uc), pltpu.roll(fx, 1, 1))
            tot = tot + flux(k[z, y0 - 1 : y0 + step - 1, :], u[z, y0 - 1 : y0 + step - 1, :])
            tot = tot + flux(k[z, y0 + 1 : y0 + step + 1, :], u[z, y0 + 1 : y0 + step + 1, :])
            if z > 0:
                tot = tot + flux(k[z - 1, y0 : y0 + step, :], u[z - 1, y0 : y0 + step, :])
            if z < nz - 1:
                tot = tot + flux(k[z + 1, y0 : y0 + step, :], u[z + 1, y0 : y0 + step, :])
            sl = slice(c * step, (c + 1) * step)
            r[z, sl, :] = r[z, sl, :] - 0.05 * uc - 0.5 * tot

    gossip()
    for side in range(2):
        @pl.when(jnp.logical_not(z_in[side]))
        def _(side=side):
            z = (0, top)[side]
            row = hrows - sent_row[side]
            far = slice(row, row + hrows)
            beyond = slice(8 + row, 8 + row + hrows)
            r[z, far, :] = r[z, far, :] - 0.5 * (k[z, beyond, :] * u[z, beyond, :])

    def r_save(z, c):
        rws = pl.ds(at(c), step)
        return pltpu.make_async_copy(r.at[z, rws, :], r_out.at[z, rws, :], out_sem.at[z, c])

    def sketch(parts):
        total = jnp.zeros((blk, blk), F32)
        for x_all, p, c in parts:
            vals = []
            for q in range(nq):
                x = x_all[:, q * blk : (q + 1) * blk]
                low = lowb[p, pl.ds(at(c), step), q * blk : (q + 1) * blk]
                bit = 1
                while bit < fine:
                    x = jnp.where((low & bit) != 0, pltpu.roll(x, bit, 1), x)
                    bit *= 2
                keep = col >= low
                vals.append(jnp.where(keep, x, 0.0))
                vals.append(jnp.where(keep, 0.0, x))
            val = jnp.concatenate(vals, 0)
            big = val.astype(BF16)
            small = (val - big.astype(F32)).astype(BF16)
            hot = hots[p, c]
            total = total + jnp.dot(hot, big, preferred_element_type=F32)
            total = total + jnp.dot(hot, small, preferred_element_type=F32)
        return total

    def early(i, total):
        parts = [(r[top, pl.ds(at(i), step), :], top, i)]
        parts.append((r[0, pl.ds(at(half + i), step), :], 0, half + i))
        for z in range(1, top):
            for c in (i, half + i):
                parts.append((r[z, pl.ds(at(c), step), :], z, c))
                r_save(z, c).start()
        return total + sketch(parts)

    total = lax.fori_loop(0, half, early, jnp.zeros((blk, blk), F32))
    gossip()
    real = [jnp.where(z_in[side], 1.0, 0.0) for side in range(2)]
    for side in range(2):
        @pl.when(z_in[side])
        def _(side=side):
            for which in range(2):
                o_send(side, which).wait_recv()
            k_send(side).wait_recv()
        prepare(nz + side, oh[side, 0], oh[side, 1], range(side * half, side * half + half))

    def finish(i, total):
        parts = []
        for side in range(2):
            z = (0, top)[side]
            c = i + side * half

            @pl.when(z_in[side])
            def _(side=side):
                u_send(side, i).wait_recv()

            uc = u[z, pl.ds(8 + at(c), step), :]
            kc = k[z, pl.ds(8 + at(c), step), :]
            rws = pl.ds(at(i), step)
            t = 0.5 * ((kc + kh[side, rws, :]) * (uc - uh[side, rws, :]))
            tf[side, rws, :] = t

            @pl.when(z_in[side])
            def _(side=side):
                f_send(side, i).start()

            res = r[z, pl.ds(at(c), step), :] - t
            r[z, pl.ds(at(c), step), :] = res
            r_save(z, c).start()
            parts.append((res, z, c))
            parts.append((t * real[side], nz + side, c))
        return total + sketch(parts)

    gossip()

    def more(i, carry):
        speak(i)
        hear(i)
        return carry

    grid[...] = lax.fori_loop(0, half, finish, total)
    lax.fori_loop(state["said"], rounds, more, 0)
    total = jnp.zeros((rows, blk), F32)
    lane = lax.broadcasted_iota(jnp.int32, (rows, blk), 1)
    for d in range(blk // fine):
        x = grid[pl.ds(d, rows, stride=blk // fine), :]
        x = pltpu.roll(x, d * fine, 1) if d else x
        total = total + jnp.where(lane >= d * fine, x, 0.0)
        if d:
            total = total + pltpu.roll(jnp.where(lane >= d * fine, 0.0, x), 1, 0)

    def settle():
        def body(i, carry):
            for side in range(2):
                z = (0, top)[side]
                c = i + (1 - side) * half

                @pl.when(z_in[side])
                def _(side=side):
                    f_send(1 - side, i).wait_recv()

                rws = pl.ds(at(c), step)
                r[z, rws, :] = r[z, rws, :] + th[side, pl.ds(at(i), step), :]
                r_save(z, c).start()
            return carry
        lax.fori_loop(0, half, body, 0)

    def reduce(mine, axis, me, count, part, slots, ssem, rsem, between):
        part[...] = mine
        slots[me] = mine

        def send(i):
            dev = lax.rem(me + i, count)
            return remote(part, slots.at[me], ssem.at[i], rsem.at[me], {axis: dev})

        def take(i):
            src = lax.rem(me + i, count)
            return remote(part, slots.at[src], ssem.at[i], rsem.at[src], {axis: src})

        def go(i, carry):
            send(i).start()
            return carry

        def land(i, carry):
            take(i).wait_recv()
            return carry

        lax.fori_loop(1, count, go, 0)
        between()
        lax.fori_loop(1, count, land, 0)
        return lax.fori_loop(0, count, lambda i, acc: acc + slots[i], jnp.zeros_like(mine))

    total = reduce(total, "gy", gy, n_gy, part_y, slots_y, s1s, s1r, lambda: None)
    total = reduce(total, "gz", gz, n_gz, part_z, slots_z, s2s, s2r, settle)
    mean = jnp.sum(total * total) / (rows * blk)
    s_out[...] = total / jnp.sqrt(jnp.full((rows, blk), mean, F32) + 1e-06)

    u_save.wait()
    for side in range(2):
        @pl.when(z_out[side])
        def _(side=side):
            k_send(side).wait_send()
            for which in range(2):
                o_send(side, which).wait_send()
            lax.fori_loop(0, half, lambda i, x: (u_send(side, i).wait_send(), x)[1], 0)

        @pl.when(z_in[side])
        def _(side=side):
            lax.fori_loop(0, half, lambda i, x: (f_send(side, i).wait_send(), x)[1], 0)

        @pl.when(y_out[side])
        def _(side=side):
            y_send(side).wait_send()

    def drain(c, carry):
        for z in range(nz):
            r_save(z, c).wait()
        return carry

    lax.fori_loop(0, nr, drain, 0)

    def sent(axis, me, count, part, slots, ssem, rsem):
        def body(i, carry):
            dev = lax.rem(me + i, count)
            remote(part, slots.at[me], ssem.at[i], rsem.at[me], {axis: dev}).wait_send()
            return carry
        lax.fori_loop(1, count, body, 0)

    sent("gy", gy, n_gy, part_y, slots_y, s1s, s1r)
    sent("gz", gz, n_gz, part_z, slots_z, s2s, s2r)


def deliver(u_in, r_in, s_in, u_out, r_out, s_out, ub, rb, in_sem, out_sem):
    pairs = []
    nz, ny, nx = u_in.shape
    n = in_sem.shape[0] // 2
    for i in range(n):
        rws = pl.ds(i * (ny // n), ny // n)
        for j, (src, buf, dst) in enumerate(((u_in, ub, u_out), (r_in, rb, r_out))):
            sem = 2 * i + j
            pairs.append((
                pltpu.make_async_copy(src.at[:, rws, :], buf.at[:, rws, :], in_sem.at[sem]),
                pltpu.make_async_copy(buf.at[:, rws, :], dst.at[:, rws, :], out_sem.at[sem]),
            ))
    for load, _ in pairs:
        load.start()
    s_out[...] = s_in[...]
    for load, store in pairs:
        load.wait()
        store.start()
    for _, store in pairs:
        store.wait()


def shards(n_gz, n_gy, iterate, basis, coeffs, rhs, kappa, offsets, flips):
    nk, nz, ny, nx = basis.shape
    nq = offsets.shape[-1]
    blk = nx // nq
    rows = SK // blk
    nr = ny // 16
    half = nr // 2
    hrows = half * 16
    dma = pltpu.SemaphoreType.DMA
    hbm = pl.BlockSpec(memory_space=pl.ANY)
    vmem = pl.BlockSpec(memory_space=pltpu.VMEM)
    shapes = (
        jax.ShapeDtypeStruct((nz, ny, nx), F32),
        jax.ShapeDtypeStruct((nz, ny, nx), F32),
        jax.ShapeDtypeStruct((rows, blk), F32),
    )
    u, r, s = pl.pallas_call(
        functools.partial(kernel, n_gz, n_gy, blk, rows),
        out_shape=shapes,
        in_specs=[pl.BlockSpec(memory_space=pltpu.SMEM), hbm, hbm, hbm, hbm, vmem, vmem],
        out_specs=(hbm, hbm, vmem),
        scratch_shapes=[
            pltpu.VMEM((nk, nz, ny, nx), BF16),
            pltpu.VMEM((nk, 16, blk), F32),
            pltpu.VMEM((nz, ny + 16, nx), F32),
            pltpu.VMEM((nz, ny + 16, nx), F32),
            pltpu.VMEM((nz, ny, nx), F32),
            pltpu.VMEM((2, hrows, nx), F32),
            pltpu.VMEM((2, hrows, nx), F32),
            pltpu.VMEM((2, hrows, nx), F32),
            pltpu.VMEM((2, hrows, nx), F32),
            pltpu.VMEM((2, 2, nq, ny), jnp.int32),
            pltpu.VMEM((nz + 2, ny, nx), jnp.int32),
            pltpu.VMEM((nz + 2, nr, blk, 2 * nq * 16), BF16),
            pltpu.VMEM((blk, blk), F32),
            pltpu.VMEM((2, 2 * nz, nx), F32),
            pltpu.VMEM((2, 2 * nz, nx), F32),
            pltpu.VMEM((n_gy, rows, blk), F32),
            pltpu.VMEM((n_gz, rows, blk), F32),
            pltpu.VMEM((rows, blk), F32),
            pltpu.VMEM((rows, blk), F32),
            dma((nz, nr)),
            dma((3,)),
            dma((2, half)),
            dma((2, half)),
            dma((2,)),
            dma((2,)),
            dma((2, half)),
            dma((2, half)),
            dma((2, 2)),
            dma((2, 2)),
            dma((2,)),
            dma((2,)),
            dma((n_gy,)),
            dma((n_gy,)),
            dma((n_gz,)),
            dma((n_gz,)),
            dma((nz, nr)),
            dma((1,)),
            pltpu.SemaphoreType.REGULAR((2, max(n_gz - 2, 1))),
        ],
        compiler_params=pltpu.CompilerParams(collective_id=0, has_side_effects=True),
    )(
        coeffs, iterate, basis, rhs, kappa,
        offsets.transpose(0, 2, 1), flips.transpose(0, 2, 1),
    )
    u, r, s = pl.pallas_call(
        deliver,
        out_shape=shapes,
        in_specs=[hbm, hbm, vmem],
        out_specs=(hbm, hbm, vmem),
        scratch_shapes=[
            pltpu.VMEM((nz, ny, nx), F32),
            pltpu.VMEM((nz, ny, nx), F32),
            dma((4,)),
            dma((4,)),
        ],
    )(u, r, s)
    return u, r, s.reshape(SK)


def solution(mesh):
    field = P("gz", "gy", None)
    return jax.shard_map(
        functools.partial(shards, mesh.shape["gz"], mesh.shape["gy"]),
        mesh=mesh,
        in_specs=(field, P(None, "gz", "gy", None), P(), field, field, field, field),
        out_specs=(field, field, P()),
        check_vma=False,
    )
```

```python
import functools

import jax
import jax.numpy as jnp
from jax import lax
from jax.experimental import pallas as pl
from jax.experimental.pallas import tpu as pltpu
from jax.sharding import PartitionSpec as P

SK = 2048
MESH = pl.DeviceIdType.MESH
F32 = jnp.float32
BF16 = jnp.bfloat16


def kernel(
    n_gz, n_gy, blk, rows,
    coef, iterate, basis, rhs, kappa, offsets, flips,
    u_out, r_out, s_out,
    bas, cf, u, k, r, uh, kh, tf, th, oh, lowb, hots, grid, ysend, yrecv,
    slots_y, slots_z, part_y, part_z,
    bas_sem, load_sem, us, ur, ks, kr, fs, fr, os_, or_, ys, yr, s1s, s1r, s2s, s2r,
    out_sem, uout_sem, near,
):
    nk, nz, ny, nx = basis.shape
    nq = nx // blk
    fine = 16
    cells = rows * blk // fine
    step = 16
    nr = ny // step
    half = nr // 2
    hrows = half * step
    assert nz >= 2 and ny == 2 * hrows and cells <= blk and blk % fine == 0
    gz = lax.axis_index("gz")
    gy = lax.axis_index("gy")
    has_dn = gz > 0
    has_up = gz < n_gz - 1
    has_lf = gy > 0
    has_rt = gy < n_gy - 1
    top = nz - 1

    def at(c):
        return pl.multiple_of(c * step, step)

    def bas_copy(z, c):
        rws = pl.ds(pl.multiple_of(c * step, step), step)
        return pltpu.make_async_copy(
            basis.at[:, z, rws, :], bas.at[:, z, rws, :], bas_sem.at[z, c]
        )

    u_load = pltpu.make_async_copy(iterate, u.at[:, pl.ds(8, ny), :], load_sem.at[0])
    k_load = pltpu.make_async_copy(kappa, k.at[:, pl.ds(8, ny), :], load_sem.at[1])
    r_load = pltpu.make_async_copy(rhs, r, load_sem.at[2])
    u_load.start()
    for i in range(half):
        bas_copy(top, i).start()
        bas_copy(0, half + i).start()
    for i in range(half):
        bas_copy(top, half + i).start()
        bas_copy(0, i).start()
        for z in range(1, top):
            bas_copy(z, i).start()
            bas_copy(z, half + i).start()
    k_load.start()
    r_load.start()

    barrier = pltpu.get_barrier_semaphore()

    def hail(axis, me, count):
        def body(i, carry):
            pl.semaphore_signal(
                barrier, inc=1, device_id={axis: lax.rem(me + i, count)}, device_id_type=MESH
            )
            return carry
        lax.fori_loop(1, count, body, 0)

    def tell(side, sem):
        @pl.when((has_up, has_dn)[side])
        def _():
            dev = lax.rem(gz + (1, n_gz - 1)[side], n_gz)
            pl.semaphore_signal(sem, inc=1, device_id={"gz": dev}, device_id_type=MESH)

    for side in range(2):
        tell(side, barrier)
    hail("gy", gy, n_gy)
    col = lax.broadcasted_iota(jnp.int32, (step, blk), 1)

    def prepare(p, off, flip, chunks):
        off = off.T
        sgn = (2 * flip - 1).astype(F32).T
        for c in chunks:
            rws = slice(c * step, (c + 1) * step)
            cols = []
            for q in range(nq):
                o = jnp.broadcast_to(off[rws, q : q + 1], (step, blk))
                s = jnp.broadcast_to(sgn[rws, q : q + 1], (step, blk))
                lowb[p, rws, q * blk : (q + 1) * blk] = o & (fine - 1)
                hi = o // fine
                nxt = hi + blk // fine
                nxt = jnp.where(nxt >= cells, nxt - cells, nxt)
                cols.append(jnp.where(col == hi, s, 0.0).astype(BF16))
                cols.append(jnp.where(col == nxt, s, 0.0).astype(BF16))
            hots[p, c] = jnp.concatenate(cols, 0).T

    for j in range(nk):
        cf[j] = jnp.full((step, blk), coef[j], F32).astype(BF16).astype(F32)
    pl.semaphore_wait(barrier, n_gy - 1 + has_up.astype(jnp.int32) + has_dn.astype(jnp.int32))

    rounds = max(n_gz - 2, 0)

    def speak(t):
        for side in range(2):
            tell(side, near.at[side, t])

    def hear(t):
        for side in range(2):
            @pl.when((has_dn, has_up)[side])
            def _(side=side):
                pl.semaphore_wait(near.at[side, t], 1)

    state = {"said": 0, "heard": 0}

    def gossip():
        if state["heard"] < state["said"]:
            hear(state["heard"])
            state["heard"] += 1
        if state["said"] < rounds:
            speak(state["said"])
            state["said"] += 1


    up = {"gz": lax.rem(gz + 1, n_gz)}
    dn = {"gz": lax.rem(gz + n_gz - 1, n_gz)}
    rt = {"gy": lax.rem(gy + 1, n_gy)}
    lf = {"gy": lax.rem(gy + n_gy - 1, n_gy)}

    def remote(src, dst, ssem, rsem, dev):
        return pltpu.make_async_remote_copy(
            src_ref=src, dst_ref=dst, send_sem=ssem, recv_sem=rsem,
            device_id=dev, device_id_type=MESH,
        )

    sent_plane = (top, 0)
    sent_row = (0, hrows)
    toward = (up, dn)

    def k_send(side):
        return remote(
            kappa.at[sent_plane[side], pl.ds(sent_row[side], hrows), :], kh.at[side],
            ks.at[side], kr.at[side], toward[side],
        )

    def o_send(side, which):
        src = (offsets, flips)[which]
        return remote(
            src.at[sent_plane[side]], oh.at[side, which],
            os_.at[side, which], or_.at[side, which], toward[side],
        )

    def u_send(side, i):
        return remote(
            u.at[sent_plane[side], pl.ds(8 + sent_row[side] + at(i), step), :],
            uh.at[side, pl.ds(at(i), step), :],
            us.at[side, i], ur.at[side, i], toward[side],
        )

    def f_send(side, i):
        return remote(
            tf.at[side, pl.ds(at(i), step), :], th.at[1 - side, pl.ds(at(i), step), :],
            fs.at[side, i], fr.at[1 - side, i], toward[1 - side],
        )

    def y_send(side):
        return remote(
            ysend.at[side], yrecv.at[side], ys.at[side], yr.at[side],
            rt if side == 0 else lf,
        )

    z_out = (has_up, has_dn)
    z_in = (has_dn, has_up)
    y_out = (has_rt, has_lf)
    y_in = (has_lf, has_rt)
    for side in range(2):
        @pl.when(z_out[side])
        def _(side=side):
            k_send(side).start()
            for which in range(2):
                o_send(side, which).start()

    gossip()

    u_load.wait()

    def combine(z, c):
        bas_copy(z, c).wait()
        acc = u[z, pl.ds(8 + at(c), step), :]
        for j in range(nk):
            cj = jnp.concatenate([cf[j]] * nq, 1)
            acc = acc + cj * bas[j, z, pl.ds(at(c), step), :].astype(F32)
        u[z, pl.ds(8 + at(c), step), :] = acc

    def first(i, carry):
        for side in range(2):
            combine(sent_plane[side], i + side * half)

            @pl.when(z_out[side])
            def _(side=side):
                u_send(side, i).start()
        return carry

    def second(i, carry):
        combine(top, half + i)
        combine(0, i)
        for z in range(1, top):
            combine(z, i)
            combine(z, half + i)
        return carry

    lax.fori_loop(0, half, first, 0)
    gossip()
    lax.fori_loop(0, half, second, 0)
    gossip()
    u_save = pltpu.make_async_copy(u.at[:, pl.ds(8, ny), :], u_out, uout_sem.at[0])
    u_save.start()
    k_load.wait()
    for side in range(2):
        row = 8 + (ny - 1 if side == 0 else 0)
        for z in range(nz):
            ysend[side, z : z + 1, :] = u[z, row : row + 1, :]
            ysend[side, nz + z : nz + z + 1, :] = k[z, row : row + 1, :]

        @pl.when(y_out[side])
        def _(side=side):
            y_send(side).start()

    for side in range(2):
        @pl.when(jnp.logical_not(z_in[side]))
        def _(side=side):
            uh[side] = jnp.zeros((hrows, nx), F32)
            kh[side] = jnp.zeros((hrows, nx), F32)
            th[side] = jnp.zeros((hrows, nx), F32)
            oh[side] = jnp.zeros((2, nq, ny), jnp.int32)

    r_load.wait()
    for side in range(2):
        row = 7 if side == 0 else 8 + ny

        @pl.when(y_in[side])
        def _(side=side, row=row):
            y_send(side).wait_recv()
            for z in range(nz):
                u[z, row : row + 1, :] = yrecv[side, z : z + 1, :]
                k[z, row : row + 1, :] = yrecv[side, nz + z : nz + z + 1, :]

        @pl.when(jnp.logical_not(y_in[side]))
        def _(row=row):
            for z in range(nz):
                u[z, row : row + 1, :] = jnp.zeros((1, nx), F32)
                k[z, row : row + 1, :] = jnp.zeros((1, nx), F32)

    for z in range(nz):
        prepare(z, offsets[z], flips[z], range(nr))
    gossip()
    lane = lax.broadcasted_iota(jnp.int32, (step, nx), 1)
    for c in range(nr):
        y0 = 8 + c * step
        for z in range(nz):
            uc = u[z, y0 : y0 + step, :]
            kc = k[z, y0 : y0 + step, :]

            def flux(ku, uu):
                return (kc + ku) * (uc - uu)

            ur_ = jnp.where(lane == nx - 1, 0.0, pltpu.roll(uc, nx - 1, 1))
            kr_ = jnp.where(lane == nx - 1, 0.0, pltpu.roll(kc, nx - 1, 1))
            fx = flux(kr_, ur_)
            tot = fx - jnp.where(lane == 0, -(kc * uc), pltpu.roll(fx, 1, 1))
            tot = tot + flux(k[z, y0 - 1 : y0 + step - 1, :], u[z, y0 - 1 : y0 + step - 1, :])
            tot = tot + flux(k[z, y0 + 1 : y0 + step + 1, :], u[z, y0 + 1 : y0 + step + 1, :])
            if z > 0:
                tot = tot + flux(k[z - 1, y0 : y0 + step, :], u[z - 1, y0 : y0 + step, :])
            if z < nz - 1:
                tot = tot + flux(k[z + 1, y0 : y0 + step, :], u[z + 1, y0 : y0 + step, :])
            sl = slice(c * step, (c + 1) * step)
            r[z, sl, :] = r[z, sl, :] - 0.05 * uc - 0.5 * tot

    gossip()
    for side in range(2):
        @pl.when(jnp.logical_not(z_in[side]))
        def _(side=side):
            z = (0, top)[side]
            row = hrows - sent_row[side]
            far = slice(row, row + hrows)
            beyond = slice(8 + row, 8 + row + hrows)
            r[z, far, :] = r[z, far, :] - 0.5 * (k[z, beyond, :] * u[z, beyond, :])

    def r_save(z, c):
        rws = pl.ds(at(c), step)
        return pltpu.make_async_copy(r.at[z, rws, :], r_out.at[z, rws, :], out_sem.at[z, c])

    def sketch(parts):
        total = jnp.zeros((blk, blk), F32)
        for x_all, p, c in parts:
            vals = []
            for q in range(nq):
                x = x_all[:, q * blk : (q + 1) * blk]
                low = lowb[p, pl.ds(at(c), step), q * blk : (q + 1) * blk]
                bit = 1
                while bit < fine:
                    x = jnp.where((low & bit) != 0, pltpu.roll(x, bit, 1), x)
                    bit *= 2
                keep = col >= low
                vals.append(jnp.where(keep, x, 0.0))
                vals.append(jnp.where(keep, 0.0, x))
            val = jnp.concatenate(vals, 0)
            big = val.astype(BF16)
            small = (val - big.astype(F32)).astype(BF16)
            hot = hots[p, c]
            total = total + jnp.dot(hot, big, preferred_element_type=F32)
            total = total + jnp.dot(hot, small, preferred_element_type=F32)
        return total

    def early(i, total):
        parts = [(r[top, pl.ds(at(i), step), :], top, i)]
        parts.append((r[0, pl.ds(at(half + i), step), :], 0, half + i))
        for z in range(1, top):
            for c in (i, half + i):
                parts.append((r[z, pl.ds(at(c), step), :], z, c))
                r_save(z, c).start()
        return total + sketch(parts)

    total = lax.fori_loop(0, half, early, jnp.zeros((blk, blk), F32))
    gossip()
    real = [jnp.where(z_in[side], 1.0, 0.0) for side in range(2)]
    for side in range(2):
        @pl.when(z_in[side])
        def _(side=side):
            for which in range(2):
                o_send(side, which).wait_recv()
            k_send(side).wait_recv()
        prepare(nz + side, oh[side, 0], oh[side, 1], range(side * half, side * half + half))

    def finish(i, total):
        parts = []
        for side in range(2):
            z = (0, top)[side]
            c = i + side * half

            @pl.when(z_in[side])
            def _(side=side):
                u_send(side, i).wait_recv()

            uc = u[z, pl.ds(8 + at(c), step), :]
            kc = k[z, pl.ds(8 + at(c), step), :]
            rws = pl.ds(at(i), step)
            t = 0.5 * ((kc + kh[side, rws, :]) * (uc - uh[side, rws, :]))
            tf[side, rws, :] = t

            res = r[z, pl.ds(at(c), step), :] - t
            r[z, pl.ds(at(c), step), :] = res
            r_save(z, c).start()
            parts.append((res, z, c))
            parts.append((t * real[side], nz + side, c))
        return total + sketch(parts)

    gossip()

    def more(i, carry):
        speak(i)
        hear(i)
        return carry

    grid[...] = lax.fori_loop(0, half, finish, total)
    lax.fori_loop(state["said"], rounds, more, 0)
    total = jnp.zeros((rows, blk), F32)
    lane = lax.broadcasted_iota(jnp.int32, (rows, blk), 1)
    for d in range(blk // fine):
        x = grid[pl.ds(d, rows, stride=blk // fine), :]
        x = pltpu.roll(x, d * fine, 1) if d else x
        total = total + jnp.where(lane >= d * fine, x, 0.0)
        if d:
            total = total + pltpu.roll(jnp.where(lane >= d * fine, 0.0, x), 1, 0)

    def settle():
        def give(i, carry):
            for side in range(2):
                @pl.when(z_in[side])
                def _(side=side):
                    f_send(side, i).start()
            return carry

        lax.fori_loop(0, half, give, 0)

        def body(i, carry):
            for side in range(2):
                z = (0, top)[side]
                c = i + (1 - side) * half

                @pl.when(z_in[side])
                def _(side=side):
                    f_send(1 - side, i).wait_recv()

                rws = pl.ds(at(c), step)
                r[z, rws, :] = r[z, rws, :] + th[side, pl.ds(at(i), step), :]
                r_save(z, c).start()
            return carry
        lax.fori_loop(0, half, body, 0)

    def reduce(mine, axis, me, count, part, slots, ssem, rsem, between):
        part[...] = mine
        slots[me] = mine

        def send(i):
            dev = lax.rem(me + i, count)
            return remote(part, slots.at[me], ssem.at[i], rsem.at[me], {axis: dev})

        def take(i):
            src = lax.rem(me + i, count)
            return remote(part, slots.at[src], ssem.at[i], rsem.at[src], {axis: src})

        def go(i, carry):
            send(i).start()
            return carry

        def land(i, carry):
            take(i).wait_recv()
            return carry

        lax.fori_loop(1, count, go, 0)
        between()
        lax.fori_loop(1, count, land, 0)
        return lax.fori_loop(0, count, lambda i, acc: acc + slots[i], jnp.zeros_like(mine))

    total = reduce(total, "gy", gy, n_gy, part_y, slots_y, s1s, s1r, lambda: None)
    total = reduce(total, "gz", gz, n_gz, part_z, slots_z, s2s, s2r, settle)
    mean = jnp.sum(total * total) / (rows * blk)
    s_out[...] = total / jnp.sqrt(jnp.full((rows, blk), mean, F32) + 1e-06)

    u_save.wait()
    for side in range(2):
        @pl.when(z_out[side])
        def _(side=side):
            k_send(side).wait_send()
            for which in range(2):
                o_send(side, which).wait_send()
            lax.fori_loop(0, half, lambda i, x: (u_send(side, i).wait_send(), x)[1], 0)

        @pl.when(z_in[side])
        def _(side=side):
            lax.fori_loop(0, half, lambda i, x: (f_send(side, i).wait_send(), x)[1], 0)

        @pl.when(y_out[side])
        def _(side=side):
            y_send(side).wait_send()

    def drain(c, carry):
        for z in range(nz):
            r_save(z, c).wait()
        return carry

    lax.fori_loop(0, nr, drain, 0)

    def sent(axis, me, count, part, slots, ssem, rsem):
        def body(i, carry):
            dev = lax.rem(me + i, count)
            remote(part, slots.at[me], ssem.at[i], rsem.at[me], {axis: dev}).wait_send()
            return carry
        lax.fori_loop(1, count, body, 0)

    sent("gy", gy, n_gy, part_y, slots_y, s1s, s1r)
    sent("gz", gz, n_gz, part_z, slots_z, s2s, s2r)


def deliver(u_in, r_in, s_in, u_out, r_out, s_out, ub, rb, in_sem, out_sem):
    pairs = []
    nz, ny, nx = u_in.shape
    n = in_sem.shape[0] // 2
    for i in range(n):
        rws = pl.ds(i * (ny // n), ny // n)
        for j, (src, buf, dst) in enumerate(((u_in, ub, u_out), (r_in, rb, r_out))):
            sem = 2 * i + j
            pairs.append((
                pltpu.make_async_copy(src.at[:, rws, :], buf.at[:, rws, :], in_sem.at[sem]),
                pltpu.make_async_copy(buf.at[:, rws, :], dst.at[:, rws, :], out_sem.at[sem]),
            ))
    for load, _ in pairs:
        load.start()
    s_out[...] = s_in[...]
    for load, store in pairs:
        load.wait()
        store.start()
    for _, store in pairs:
        store.wait()


def shards(n_gz, n_gy, iterate, basis, coeffs, rhs, kappa, offsets, flips):
    nk, nz, ny, nx = basis.shape
    nq = offsets.shape[-1]
    blk = nx // nq
    rows = SK // blk
    nr = ny // 16
    half = nr // 2
    hrows = half * 16
    dma = pltpu.SemaphoreType.DMA
    hbm = pl.BlockSpec(memory_space=pl.ANY)
    vmem = pl.BlockSpec(memory_space=pltpu.VMEM)
    shapes = (
        jax.ShapeDtypeStruct((nz, ny, nx), F32),
        jax.ShapeDtypeStruct((nz, ny, nx), F32),
        jax.ShapeDtypeStruct((rows, blk), F32),
    )
    u, r, s = pl.pallas_call(
        functools.partial(kernel, n_gz, n_gy, blk, rows),
        out_shape=shapes,
        in_specs=[pl.BlockSpec(memory_space=pltpu.SMEM), hbm, hbm, hbm, hbm, vmem, vmem],
        out_specs=(hbm, hbm, vmem),
        scratch_shapes=[
            pltpu.VMEM((nk, nz, ny, nx), BF16),
            pltpu.VMEM((nk, 16, blk), F32),
            pltpu.VMEM((nz, ny + 16, nx), F32),
            pltpu.VMEM((nz, ny + 16, nx), F32),
            pltpu.VMEM((nz, ny, nx), F32),
            pltpu.VMEM((2, hrows, nx), F32),
            pltpu.VMEM((2, hrows, nx), F32),
            pltpu.VMEM((2, hrows, nx), F32),
            pltpu.VMEM((2, hrows, nx), F32),
            pltpu.VMEM((2, 2, nq, ny), jnp.int32),
            pltpu.VMEM((nz + 2, ny, nx), jnp.int32),
            pltpu.VMEM((nz + 2, nr, blk, 2 * nq * 16), BF16),
            pltpu.VMEM((blk, blk), F32),
            pltpu.VMEM((2, 2 * nz, nx), F32),
            pltpu.VMEM((2, 2 * nz, nx), F32),
            pltpu.VMEM((n_gy, rows, blk), F32),
            pltpu.VMEM((n_gz, rows, blk), F32),
            pltpu.VMEM((rows, blk), F32),
            pltpu.VMEM((rows, blk), F32),
            dma((nz, nr)),
            dma((3,)),
            dma((2, half)),
            dma((2, half)),
            dma((2,)),
            dma((2,)),
            dma((2, half)),
            dma((2, half)),
            dma((2, 2)),
            dma((2, 2)),
            dma((2,)),
            dma((2,)),
            dma((n_gy,)),
            dma((n_gy,)),
            dma((n_gz,)),
            dma((n_gz,)),
            dma((nz, nr)),
            dma((1,)),
            pltpu.SemaphoreType.REGULAR((2, max(n_gz - 2, 1))),
        ],
        compiler_params=pltpu.CompilerParams(collective_id=0, has_side_effects=True),
    )(
        coeffs, iterate, basis, rhs, kappa,
        offsets.transpose(0, 2, 1), flips.transpose(0, 2, 1),
    )
    u, r, s = pl.pallas_call(
        deliver,
        out_shape=shapes,
        in_specs=[hbm, hbm, vmem],
        out_specs=(hbm, hbm, vmem),
        scratch_shapes=[
            pltpu.VMEM((nz, ny, nx), F32),
            pltpu.VMEM((nz, ny, nx), F32),
            dma((4,)),
            dma((4,)),
        ],
    )(u, r, s)
    return u, r, s.reshape(SK)


def solution(mesh):
    field = P("gz", "gy", None)
    return jax.shard_map(
        functools.partial(shards, mesh.shape["gz"], mesh.shape["gy"]),
        mesh=mesh,
        in_specs=(field, P(None, "gz", "gy", None), P(), field, field, field, field),
        out_specs=(field, field, P()),
        check_vma=False,
    )
```
